128 devices in a mesh: row: 8 (over y, core), col: 16 (over x, z).
Axes of the slice: x: 4, y: 4, z: 4, core: 2. Of those that a mesh axis runs over, the one named last changes fastest.
Arguments:
- atom_rows: bfloat16 [48, 8192, 128], P(None, ('row', 'col')), may hold values from -48 to 48
- pair_rep: bfloat16 [1024, 1024, 128], P('row', 'col'), may hold values from -6 to 6
- query_gate_weight: bfloat16 [128, 256], replicated, may hold values from -0.5 to 0.5
- key_value_weight: bfloat16 [128, 256], replicated, may hold values from -0.5 to 0.5
- output_weight: bfloat16 [128, 128], replicated, may hold values from -2 to 2
- pair_weight: float32 [128, 4], replicated, may hold values from -0.5 to 0.5
- counts: int32 [128, 8], replicated, may hold values from 1 to 24, 64 in all within a row
- token_mask: int32 [1024], replicated, may hold values 0 or 1
- cotangent: bfloat16 [48, 8192, 128], P(None, ('row', 'col')), may hold values from -6 to 6
Outputs:
- updated_atoms: bfloat16 [48, 8192, 128], P(None, ('row', 'col'))
- atom_grad: bfloat16 [48, 8192, 128], P(None, ('row', 'col'))
- pair_grad: bfloat16 [1024, 1024, 128], P('row', 'col')
- pair_weight_grad: float32 [128, 4], replicated
The draws below stay inside these ranges and needn't reach their ends.
Inputs may be any that keep to these rules, and one draw needn't show every extreme that they name: Each row of counts sums to 64, so the atoms of one aligned block of 8 tokens are one aligned block of 64 atoms; the largest entry of each row is 24.
All inputs are finite; a program needn't handle non-finite values.
Results may differ from the reference program's by a relative error of at most 0.028.
Values may be sent and summed in bfloat16 or wider, within the bound.
A program may use at most 128 MiB of HBM per device.

```python
import math
from functools import partial
import jax
import jax.numpy as jnp
import numpy as np
from jax import lax

SAMPLES = 48
ATOM_DEV = 64
TOK_DEV = 8
ATOM_CH = 128
PAIR_CH = 128
HEADS = 4
WIN_QUERY = 32
WIN_KEY = 128
MOST = 24
HALO = 48
ATOMS = 8192
TOKENS = 1024
DEVICES = 128


def draw_atom_rows(key, part):
    base_key = jax.random.fold_in(key, 0)
    return jnp.clip(jax.random.normal(base_key, (SAMPLES, ATOMS, ATOM_CH), jnp.float32), -6.0, 6.0).astype(jnp.bfloat16)


def plant(entries, own_key, smallest, high):
    shape = entries.shape
    index_at = [jax.random.randint(jax.random.fold_in(own_key, axis), (), 0, shape[axis]) for axis in range(len(shape))]
    entries = entries.at[tuple(index_at)].set(smallest)
    longest = shape.index(max(shape))
    index_at[longest] = (index_at[longest] + 1) % shape[longest]
    return entries.at[tuple(index_at)].set(high)


def steps_of(key, dims, shards, low, largest):
    loudness = 1.0
    for position, parts in shards:
        draws = jax.random.uniform(jax.random.fold_in(jax.random.fold_in(key, 6), position), (parts,), jnp.float32, low / len(shards), largest / len(shards))
        loudness = loudness * jnp.repeat(jnp.exp(draws), dims[position] // parts).reshape((-1,) + (1,) * (len(dims) - 1 - position))
    return loudness


def split_up(number_of, total, most, skew):
    loads = [(1 << 20) // math.isqrt(rank ** skew) + 1 for rank in range(2, number_of + 1)]
    rest, holding = total - most - (number_of - 1), [1] * (number_of - 1)
    while rest > 0:
        free = [i for i in range(number_of - 1) if holding[i] < most]
        whole, budget = sum([loads[i] for i in free]), rest
        for i in free:
            addition = min(most - holding[i], max(1, budget * loads[i] // whole), rest)
            holding[i] = holding[i] + addition
            rest = rest - addition
    return np.array([most] + holding)


def ragged_sizes(stream_key, number_of, total, limit, lean):
    if number_of == 2:
        one = jax.random.randint(stream_key, (), max(1, total - limit), min(limit, total - 1) + 1)
        return jnp.stack([one, total - one])
    lengths = jnp.asarray(split_up(number_of, total, limit, lean), jnp.int32)
    couples = (number_of - 1) // 2
    giver, receiver = lengths[1:1 + 2 * couples:2], lengths[2:2 + 2 * couples:2]
    room = jnp.minimum(giver - 1, limit - receiver)
    shifted = jax.random.randint(jax.random.fold_in(stream_key, 1), (couples,), 0, 1 << 20) % (room + 1)
    lengths = lengths.at[1:1 + 2 * couples:2].set(giver - shifted).at[2:2 + 2 * couples:2].set(receiver + shifted)
    return lengths[jax.random.permutation(jax.random.fold_in(stream_key, 2), number_of)]


def bell_draw(stream_key, shape, deviation, most, cuts=(), kind=jnp.bfloat16):
    factor_of = steps_of(stream_key, shape, cuts, -0.22, 0.18) if cuts else 1.0
    result = jax.random.normal(stream_key, shape, jnp.float32) * deviation * factor_of
    return jnp.minimum(jnp.maximum(result, -most), most).astype(kind)


def setup_inputs(seed: int = 0) -> dict:
    streams_of = jax.random.split(jax.random.key(seed), 10)
    return {
        "atom_rows": draw_atom_rows(jax.random.fold_in(streams_of[9], 71), 0),
        "pair_rep": bell_draw(streams_of[1], (TOKENS, TOKENS, PAIR_CH), 1.0, 6.0, ((0, 8), (1, 16))),
        "query_gate_weight": bell_draw(streams_of[2], (ATOM_CH, 2 * ATOM_CH), ATOM_CH ** -0.5, 0.5),
        "key_value_weight": bell_draw(streams_of[3], (ATOM_CH, 2 * ATOM_CH), ATOM_CH ** -0.5, 0.5),
        "output_weight": bell_draw(streams_of[4], (ATOM_CH, ATOM_CH), (ATOM_CH // 16) ** -0.5, 2.0),
        "pair_weight": bell_draw(streams_of[5], (PAIR_CH, HEADS), PAIR_CH ** -0.5, 0.5, (), jnp.float32),
        "counts": jax.vmap(lambda own: ragged_sizes(own, TOK_DEV, ATOM_DEV, MOST, 2))(jax.random.split(streams_of[6], DEVICES)).reshape((DEVICES, TOK_DEV)).astype(jnp.int32),
        "token_mask": plant((jax.random.randint(streams_of[7], (TOKENS,), 0, 8) < 7).astype(jnp.int32), jax.random.fold_in(streams_of[7], 1), 0, 1),
        "cotangent": bell_draw(streams_of[8], (SAMPLES, ATOMS, ATOM_CH), 1.0, 6.0, ((1, 128),)),
    }


EPS = 1e-05
MASKED = -1000000000.0

def group_tokens(running, group_id):
    clipped = jnp.clip(group_id, 0, running.shape[0] - 1).astype(jnp.int32)
    totals = lax.dynamic_index_in_dim(running, clipped, 0, keepdims=False)
    positions = jnp.arange(ATOM_DEV, dtype=jnp.int32)
    return lax.optimization_barrier(jnp.sum((totals[None, :] <= positions[:, None]).astype(jnp.int32), axis=1))

def layout(counts, token_mask, group_id):
    running = jnp.cumsum(counts, axis=1).astype(jnp.int32)
    own_tokens = group_tokens(running, group_id)
    preceding = group_tokens(running, group_id - 1)[ATOM_DEV - HALO:]
    following = group_tokens(running, group_id + 1)[:HALO]
    band_cols = jnp.concatenate([preceding, own_tokens + TOK_DEV, following + 2 * TOK_DEV])
    query_hot = (own_tokens[:, None] == jnp.arange(TOK_DEV, dtype=jnp.int32)[None, :]).astype(jnp.float32)
    key_matches = band_cols[:, None] == jnp.arange(3 * TOK_DEV, dtype=jnp.int32)[None, :]
    key_hot = key_matches.astype(jnp.float32)
    padded_mask = jnp.pad(token_mask, (TOK_DEV, TOK_DEV))
    band_mask = lax.dynamic_slice(padded_mask, (group_id * TOK_DEV,), (3 * TOK_DEV,))
    key_valid = lax.optimization_barrier(jnp.sum(key_matches.astype(jnp.int32) * band_mask[None, :], axis=1))
    return (query_hot, key_hot, key_valid)

def pair_band(pair_values, group_id):
    zero_index = jnp.zeros((), jnp.int32)
    blocks = []
    for step_col in (-1, 0, 1):
        col_group = group_id + step_col
        col_start = (jnp.clip(col_group, 0, DEVICES - 1) * TOK_DEV).astype(jnp.int32)
        row_start = (group_id * TOK_DEV).astype(jnp.int32)
        block = lax.dynamic_slice(pair_values, (row_start, col_start, zero_index), (TOK_DEV, TOK_DEV, PAIR_CH))
        inside = jnp.logical_and(col_group >= 0, col_group < DEVICES)
        blocks.append(jnp.where(inside, block, jnp.zeros_like(block)))
    return jnp.concatenate(blocks, axis=1)

def project_pair(block, pair_weight):
    values = block.astype(jnp.float32)
    channel_mean = lax.optimization_barrier(jnp.mean(values, axis=-1, keepdims=True))
    centered = values - channel_mean
    variance = lax.optimization_barrier(jnp.mean(centered * centered, axis=-1, keepdims=True))
    normed = centered * lax.rsqrt(variance + EPS)
    projected = jnp.einsum('...tuc,ch->...htu', normed, pair_weight, precision=lax.Precision.HIGHEST)
    return projected.astype(jnp.bfloat16)

def attend(own_rows, key_value_rows, band_bias, query_hot, key_hot, key_valid, query_gate_weight, output_weight):
    samples = own_rows.shape[0]
    channels = own_rows.shape[2]
    head_size = channels // HEADS
    flat_rows = own_rows.reshape(samples * ATOM_DEV, channels)
    query_gate = jnp.dot(flat_rows, query_gate_weight, preferred_element_type=jnp.float32)
    query_gate = query_gate.reshape(samples, ATOM_DEV, 2 * channels)
    queries = query_gate[:, :, :channels].astype(jnp.bfloat16)
    gate_value = jax.nn.sigmoid(query_gate[:, :, channels:])
    spread = jnp.einsum('htu,eu->hte', band_bias.astype(jnp.float32), key_hot)
    atom_bias = jnp.einsum('at,hte->hae', query_hot, spread)
    penalty = jnp.where(key_valid > 0, 0.0, MASKED).astype(jnp.float32)
    score_scale = 1.0 / math.sqrt(head_size)
    blocks = []
    for window in range(ATOM_DEV // WIN_QUERY):
        window_start = window * WIN_QUERY
        query_win = queries[:, window_start:window_start + WIN_QUERY].reshape(samples, WIN_QUERY, HEADS, head_size)
        key_win = key_value_rows[:, window_start:window_start + WIN_KEY, :channels].reshape(samples, WIN_KEY, HEADS, head_size)
        value_win = key_value_rows[:, window_start:window_start + WIN_KEY, channels:].reshape(samples, WIN_KEY, HEADS, head_size)
        scores = jnp.einsum('sqhd,skhd->shqk', query_win.astype(jnp.float32), key_win.astype(jnp.float32)) * score_scale
        scores = scores + atom_bias[None, :, window_start:window_start + WIN_QUERY, window_start:window_start + WIN_KEY]
        scores = scores + penalty[window_start:window_start + WIN_KEY]
        row_max = lax.stop_gradient(lax.optimization_barrier(jnp.max(scores, axis=-1, keepdims=True)))
        exponent = jnp.exp(scores - row_max)
        weights = (exponent / lax.optimization_barrier(jnp.sum(exponent, axis=-1, keepdims=True))).astype(jnp.bfloat16)
        mixed_rows = jnp.einsum('shqk,skhd->sqhd', weights.astype(jnp.float32), value_win.astype(jnp.float32))
        blocks.append(mixed_rows.reshape(samples, WIN_QUERY, channels))
    attended = jnp.concatenate(blocks, axis=1)
    gated = (attended * gate_value).astype(jnp.bfloat16)
    projected = jnp.dot(gated.reshape(samples * ATOM_DEV, channels), output_weight, preferred_element_type=jnp.float32)
    return (own_rows.astype(jnp.float32) + projected.reshape(samples, ATOM_DEV, channels)).astype(jnp.bfloat16)

def reference(atom_rows, pair_rep, query_gate_weight, key_value_weight, output_weight, pair_weight, counts, token_mask, cotangent):
    group_ids = jnp.arange(DEVICES, dtype=jnp.int32)
    query_hot, key_hot, key_valid = jax.vmap(partial(layout, counts, token_mask))(group_ids)

    def one_group(packed):
        ext_rows, bias_rows, group_query, group_key, group_valid = packed
        key_value_rows = jnp.dot(ext_rows.reshape(-1, ATOM_CH), key_value_weight, preferred_element_type=jnp.float32)
        key_value_rows = key_value_rows.reshape(SAMPLES, ATOM_DEV + 2 * HALO, 2 * ATOM_CH).astype(jnp.bfloat16)
        own_rows = ext_rows[:, HALO:HALO + ATOM_DEV]
        return attend(own_rows, key_value_rows, bias_rows, group_query, group_key, group_valid, query_gate_weight, output_weight)

    def forward(atom_values, pair_values, pair_values_weight):
        wide_rows = atom_values.astype(jnp.float32).reshape(SAMPLES, DEVICES, ATOM_DEV, ATOM_CH)
        edge_rows = jnp.zeros((SAMPLES, 1, HALO, ATOM_CH), jnp.float32)
        preceding = jnp.concatenate([edge_rows, wide_rows[:, :-1, ATOM_DEV - HALO:]], axis=1)
        following = jnp.concatenate([wide_rows[:, 1:, :HALO], edge_rows], axis=1)
        extended = jnp.concatenate([preceding, wide_rows, following], axis=2).astype(jnp.bfloat16)
        bands = jax.vmap(partial(pair_band, pair_values))(group_ids)
        band_bias = project_pair(bands, pair_values_weight)
        outputs = lax.map(jax.checkpoint(one_group), (jnp.moveaxis(extended, 1, 0), band_bias, query_hot, key_hot, key_valid))
        return jnp.moveaxis(outputs, 0, 1).reshape(SAMPLES, ATOMS, ATOM_CH)
    updated_atoms, pullback = jax.vjp(forward, atom_rows, pair_rep, pair_weight)
    atom_grad, pair_grad, pair_weight_grad = pullback(cotangent)
    return (updated_atoms, atom_grad, pair_grad, pair_weight_grad)
```

```python
import functools
import math

import jax
import jax.numpy as jnp
from jax import lax
from jax.experimental import pallas as pl
from jax.experimental.pallas import tpu as pltpu
from jax.sharding import PartitionSpec as P

BLOCK = 64
TOK = 8
HEADS = 4
WIN = 32
KEYS = 128
HALO = 48
CH = 128
EXT = BLOCK + 2 * HALO
LANES = 2 * HEADS * WIN
EPS = 1e-05
MASKED = -1000000000.0
SCALE = 1.0 / math.sqrt(CH // HEADS)
STEP = 4
AHEAD = 3
LAG = 4
DELAY = 4
HALF = 2

F32 = jnp.float32
BF16 = jnp.bfloat16
HI = lax.Precision.HIGHEST
MESH = pl.DeviceIdType.MESH


def nn(a, b, precision=None):
    return lax.dot_general(a, b, (((1,), (0,)), ((), ())), precision=precision, preferred_element_type=F32)


def nt(a, b, precision=None):
    return lax.dot_general(a, b, (((1,), (1,)), ((), ())), precision=precision, preferred_element_type=F32)


def tn(a, b, precision=None):
    return lax.dot_general(a, b, (((0,), (0,)), ((), ())), precision=precision, preferred_element_type=F32)


def iota(shape, dim):
    return lax.broadcasted_iota(jnp.int32, shape, dim)


def normalize(values):
    centered = values - jnp.mean(values, axis=1, keepdims=True)
    rstd = lax.rsqrt(jnp.mean(centered * centered, axis=1, keepdims=True) + EPS)
    return centered * rstd, rstd


def totals_of(counts, group):
    running, total = [], 0
    for j in range(TOK):
        total = total + counts[j, group]
        running.append(total)
    return running


def main_kernel(
    rows, cols, samples,
    counts_hbm, mask_hbm, x_hbm, pair_hbm, wqg_hbm, wkv_hbm, wo_hbm, pw_hbm, dy_hbm,
    upd_v, grad_v, pair_out, wgrad_out,
    counts, mask, wqg_ref, wkv_ref, wo_ref, pwt_v, pw_v,
    x_v, dy_v, lo_v, hi_v, glo_v, ghi_v, gprev_v, gnext_v, center_v,
    band_v, bandgrad_v, piece_v, bt_v, dbt_v, kv_v, dkv_v, q_v, gate_v, dgated_v, gated_v, dgate_v, dq_v,
    datt_v, prob_v, dscore_v, logit_v, dprob_v,
    red_a, red_b, part_a, part_b,
    in_sem, lo_send, hi_send, lo_recv, hi_recv, glo_send, ghi_send, gp_recv, gn_recv,
    band_send, band_recv, piece_send, piece_recv, a_send, a_recv, b_send, b_recv,
):
    chunks = samples // STEP
    blocks = rows * cols
    row = lax.axis_index("row")
    col = lax.axis_index("col")
    me = row * cols + col
    has_prev = me > 0
    has_next = me < blocks - 1
    before = jnp.maximum(me - 1, 0)
    after = jnp.minimum(me + 1, blocks - 1)
    prev_id = (before // cols, before % cols)
    next_id = (after // cols, after % cols)

    barrier = pltpu.get_barrier_semaphore()

    @pl.loop(1, cols)
    def _(d):
        pl.semaphore_signal(barrier, inc=1, device_id=(row, lax.rem(col + d, cols)), device_id_type=MESH)

    @pl.loop(1, rows)
    def _(d):
        pl.semaphore_signal(barrier, inc=1, device_id=(lax.rem(row + d, rows), col), device_id_type=MESH)

    far_next = jnp.logical_and(col == cols - 1, has_next)
    far_prev = jnp.logical_and(col == 0, has_prev)

    @pl.when(far_next)
    def _():
        pl.semaphore_signal(barrier, inc=1, device_id=next_id, device_id_type=MESH)

    @pl.when(far_prev)
    def _():
        pl.semaphore_signal(barrier, inc=1, device_id=prev_id, device_id_type=MESH)

    small_in = [
        pltpu.make_async_copy(src, dst, in_sem.at[n])
        for n, (src, dst) in enumerate([(counts_hbm, counts), (mask_hbm, mask), (pw_hbm, pwt_v)])
    ]
    large_in = [
        pltpu.make_async_copy(src, dst, in_sem.at[3 + n])
        for n, (src, dst) in enumerate(
            [(wkv_hbm, wkv_ref), (wqg_hbm, wqg_ref), (wo_hbm, wo_ref), (x_hbm, x_v), (dy_hbm, dy_v)])
    ]
    for copy in small_in + large_in:
        copy.start()

    @pl.when(jnp.logical_not(has_prev))
    def _():
        lo_v[...] = jnp.zeros_like(lo_v)
        gprev_v[...] = jnp.zeros_like(gprev_v)
        band_v[:, :TOK] = jnp.zeros((TOK, TOK, CH), BF16)

    @pl.when(jnp.logical_not(has_next))
    def _():
        hi_v[...] = jnp.zeros_like(hi_v)
        gnext_v[...] = jnp.zeros_like(gnext_v)
        band_v[:, 2 * TOK :] = jnp.zeros((TOK, TOK, CH), BF16)

    for copy in small_in:
        copy.wait()

    g_prev = jnp.maximum(me - 1, 0)
    g_next = jnp.minimum(me + 1, blocks - 1)
    run_prev, run_own, run_next = totals_of(counts, g_prev), totals_of(counts, me), totals_of(counts, g_next)
    atom = iota((EXT, 32), 0)
    is_lo, is_hi = atom < HALO, atom >= HALO + BLOCK
    local = jnp.where(is_lo, atom + (BLOCK - HALO), jnp.where(is_hi, atom - (HALO + BLOCK), atom - HALO))
    token = jnp.where(is_lo, 0, jnp.where(is_hi, 2 * TOK, TOK))
    for j in range(TOK):
        limit = jnp.where(is_lo, run_prev[j], jnp.where(is_hi, run_next[j], run_own[j]))
        token = token + (limit <= local).astype(jnp.int32)
    key_hot32 = (token == iota((EXT, 32), 1)).astype(F32)
    key_hot = key_hot32.astype(BF16)

    lane = iota((TOK, LANES), 1)
    query = (lane // KEYS) * WIN + lane % WIN
    query_token = jnp.zeros((TOK, LANES), jnp.int32)
    for j in range(TOK):
        query_token = query_token + (run_own[j] <= query).astype(jnp.int32)

    slot_row = iota((32, LANES), 0)
    mask_rows = jnp.zeros((32, LANES), F32)
    for u in range(3 * TOK):
        where_to = me * TOK + u - TOK
        bit = mask[jnp.clip(where_to, 0, blocks * TOK - 1)]
        bit = jnp.where(jnp.logical_and(where_to >= 0, where_to < blocks * TOK), bit, 0)
        mask_rows = jnp.where(slot_row == u, bit.astype(F32), mask_rows)
    valid = nn(key_hot, mask_rows.astype(BF16))

    pl.semaphore_wait(
        barrier, (cols - 1) + (rows - 1) + far_next.astype(jnp.int32) + far_prev.astype(jnp.int32)
    )

    def to_next(i):
        return pltpu.make_async_remote_copy(
            src_ref=x_hbm.at[pl.ds(i * STEP, STEP), pl.ds(BLOCK - HALO, HALO)],
            dst_ref=lo_v.at[pl.ds(i * STEP, STEP)],
            send_sem=lo_send.at[i], recv_sem=lo_recv.at[i],
            device_id=next_id, device_id_type=MESH)

    def to_prev(i):
        return pltpu.make_async_remote_copy(
            src_ref=x_hbm.at[pl.ds(i * STEP, STEP), pl.ds(0, HALO)],
            dst_ref=hi_v.at[pl.ds(i * STEP, STEP)],
            send_sem=hi_send.at[i], recv_sem=hi_recv.at[i],
            device_id=prev_id, device_id_type=MESH)

    def grad_to_prev(i):
        return pltpu.make_async_remote_copy(
            src_ref=glo_v.at[pl.ds(i * STEP, STEP)],
            dst_ref=gnext_v.at[pl.ds(i * STEP, STEP)],
            send_sem=glo_send.at[i], recv_sem=gn_recv.at[i],
            device_id=prev_id, device_id_type=MESH)

    def grad_to_next(i):
        return pltpu.make_async_remote_copy(
            src_ref=ghi_v.at[pl.ds(i * STEP, STEP)],
            dst_ref=gprev_v.at[pl.ds(i * STEP, STEP)],
            send_sem=ghi_send.at[i], recv_sem=gp_recv.at[i],
            device_id=next_id, device_id_type=MESH)

    delta = rows * col - cols * row

    def inside(j):
        return jnp.logical_and(j >= 0, j < cols)

    def clamped(j):
        return jnp.clip(j, 0, cols - 1)

    def band_refs(d, j, wide, first):
        k = d - 1 + first
        return (
            pair_hbm.at[pl.ds(j * TOK, TOK), pl.ds(pl.multiple_of(k * TOK, TOK), wide * TOK)],
            band_v.at[:, pl.ds(first * TOK, wide * TOK)])

    def band_copy(d, j, wide, first):
        src, dst = band_refs(d, j, wide, first)
        return pltpu.make_async_remote_copy(
            src_ref=src, dst_ref=dst,
            send_sem=band_send.at[d + 1], recv_sem=band_recv.at[0 if wide > 1 else 1],
            device_id=(row, j), device_id_type=MESH)

    def band_local(d, j, wide, first):
        src, dst = band_refs(d, j, wide, first)
        return pltpu.make_async_copy(src, dst, band_send.at[d + 1])

    def send_band(d, wide, first):
        j = delta + d

        @pl.when(jnp.logical_and(inside(j), j != col))
        def _():
            band_copy(d, clamped(j), wide, first).start()

        @pl.when(jnp.logical_and(inside(j), j == col))
        def _():
            band_local(d, clamped(j), wide, first).start()

    def band_sent(d, wide, first):
        j = delta + d

        @pl.when(jnp.logical_and(inside(j), j != col))
        def _():
            band_copy(d, clamped(j), wide, first).wait_send()

    def all_readers(act):
        @pl.loop(1, rows - 1)
        def _(d):
            act(d, 3, 0)

        act(0, 2, 1)
        act(rows - 1, 2, 0)
        act(-1, 1, 2)
        act(rows, 1, 0)

    owner = me // rows
    mine = me % rows
    side_low = jnp.logical_and(mine == 0, has_prev)
    side_high = jnp.logical_and(mine == rows - 1, has_next)

    def receive_band(cond, source, d, wide, first):
        @pl.when(jnp.logical_and(cond, source != col))
        def _():
            band_copy(d, col, wide, first).wait_recv()

        @pl.when(jnp.logical_and(cond, source == col))
        def _():
            band_local(d, col, wide, first).wait()

    def piece_copy(target, d, wide, first):
        at = pl.ds(first * TOK, wide * TOK)
        return pltpu.make_async_remote_copy(
            src_ref=bandgrad_v.at[:, at], dst_ref=piece_v.at[d + 1, :, at],
            send_sem=piece_send.at[0 if wide > 1 else 1], recv_sem=piece_recv.at[d + 1],
            device_id=(row, target), device_id_type=MESH)

    def to_owners(act):
        act(jnp.logical_and(mine > 0, mine < rows - 1), owner, mine, 3, 0)
        act(mine == 0, owner, 0, 2, 1)
        act(mine == rows - 1, owner, rows - 1, 2, 0)
        act(side_high, owner + 1, -1, 1, 2)
        act(side_low, owner - 1, rows, 1, 0)

    def send_rows(i):
        @pl.when(has_next)
        def _():
            to_next(i).start()

        @pl.when(has_prev)
        def _():
            to_prev(i).start()

    send_rows(0)
    all_readers(send_band)

    @pl.loop(1, AHEAD)
    def _(i):
        send_rows(i)

    to_owners(receive_band)

    def band_normed():
        return normalize(
            jnp.concatenate(
                [band_v[t, s * TOK : (s + 1) * TOK].astype(F32) for s in range(3) for t in range(TOK)], axis=0))

    pw_v[...] = jnp.concatenate([pwt_v[...], jnp.zeros((8 - HEADS, CH), F32)], axis=0).T
    head_lane = (iota((CH, LANES), 1) % KEYS) // WIN
    spread_weight = jnp.zeros((CH, LANES), F32)
    for h in range(HEADS):
        spread_weight = jnp.where(head_lane == h, pw_v[:, h : h + 1], spread_weight)
    normed, _ = band_normed()
    projected = nn(normed, spread_weight, HI)
    table = []
    for s in range(3):
        part = jnp.zeros((TOK, LANES), F32)
        for t in range(TOK):
            at = (s * TOK + t) * TOK
            part = jnp.where(query_token == t, projected[at : at + TOK], part)
        table.append(part)
    table = jnp.concatenate(table, axis=0)
    table = jnp.concatenate([table, jnp.zeros((8, LANES), F32)], axis=0).astype(BF16)
    bias = jnp.where(valid > 0.5, nn(key_hot, table), nn(key_hot, table) + MASKED)
    for w in range(2):
        bt_v[w] = bias[w * WIN : w * WIN + KEYS, w * KEYS : (w + 1) * KEYS]
    dbt_v[...] = jnp.zeros_like(dbt_v)
    pair_out[...] = jnp.zeros_like(pair_out)

    head_of = iota((WIN, CH), 1) // WIN
    head_mask = [(head_of == h).astype(BF16) for h in range(HEADS)]

    def expand(a):
        return jnp.concatenate(
            [a[w * WIN : (w + 1) * WIN] * head_mask[h] for w in range(2) for h in range(HEADS)], axis=0)

    def fold(a):
        out = a[:WIN]
        for h in range(1, HEADS):
            out = jnp.where(head_of == h, a[h * WIN : (h + 1) * WIN], out)
        return out

    gap = jnp.zeros((WIN, KEYS), BF16)

    def both(a0, a1):
        return jnp.concatenate(
            [jnp.concatenate([a0, gap], axis=0), jnp.concatenate([gap, a1], axis=0)], axis=1)

    for copy in large_in:
        copy.wait()

    def finish(i):
        @pl.when(has_next)
        def _():
            grad_to_prev(i).wait_recv()

        @pl.when(has_prev)
        def _():
            grad_to_next(i).wait_recv()

        part = pl.ds(i * STEP, STEP)
        from_prev = gprev_v[part].astype(F32)
        from_next = gnext_v[part].astype(F32)
        cut = BLOCK - HALO
        grad_v[part, 0:cut] = (center_v[part, 0:cut] + from_prev[:, :cut]).astype(BF16)
        grad_v[part, cut:HALO] = (
            center_v[part, cut:HALO] + from_prev[:, cut:] + from_next[:, : HALO - cut]).astype(BF16)
        grad_v[part, HALO:BLOCK] = (center_v[part, HALO:BLOCK] + from_next[:, HALO - cut :]).astype(BF16)

    def first_pass(i):
        @pl.when(i + AHEAD < chunks)
        def _():
            send_rows(i + AHEAD)

        part = pl.ds(i * STEP, STEP)
        x3 = x_v[part]
        x = x3.reshape(STEP * BLOCK, CH)
        dy = dy_v[part].reshape(STEP * BLOCK, CH)
        query_gate = nn(x, wqg_ref[...])
        q_v[part] = query_gate[:, :CH].astype(BF16).reshape(STEP, BLOCK, CH)
        gate_v[...] = jax.nn.sigmoid(query_gate[:, CH:]).reshape(STEP, BLOCK, CH)
        dgated_v[...] = nt(dy, wo_ref[...]).astype(BF16).reshape(STEP, BLOCK, CH)
        kv_v[part, HALO : HALO + BLOCK] = nn(x, wkv_ref[...]).astype(BF16).reshape(STEP, BLOCK, 2 * CH)

        @pl.when(has_prev)
        def _():
            to_next(i).wait_recv()

        @pl.when(has_next)
        def _():
            to_prev(i).wait_recv()

        lo = lo_v[part].reshape(STEP * HALO, CH)
        hi = hi_v[part].reshape(STEP * HALO, CH)
        kv_v[part, :HALO] = nn(lo, wkv_ref[...]).astype(BF16).reshape(STEP, HALO, 2 * CH)
        kv_v[part, HALO + BLOCK :] = nn(hi, wkv_ref[...]).astype(BF16).reshape(STEP, HALO, 2 * CH)

        for s in range(STEP):
            at = i * STEP + s
            datt = (dgated_v[s].astype(F32) * gate_v[s]).astype(BF16)
            datt_v[at] = datt
            logit_v[s] = nt(kv_v[at, :, :CH], expand(q_v[at]))
            dprob_v[s] = nt(kv_v[at, :, CH:], expand(datt))
        for w in range(2):
            ks = slice(w * WIN, w * WIN + KEYS)
            ls = slice(w * KEYS, (w + 1) * KEYS)
            for s in range(STEP):
                at = i * STEP + s
                score = logit_v[s, ks, ls] * SCALE + bt_v[w]
                e = jnp.exp(score - jnp.max(score, axis=0, keepdims=True))
                p = e * (1.0 / jnp.sum(e, axis=0, keepdims=True))
                t = dprob_v[s, ks, ls] * p
                ds = t - p * jnp.sum(t, axis=0, keepdims=True)
                dbt_v[w] += ds
                prob_v[at, w] = p.astype(BF16)
                dscore_v[at, w] = ds.astype(BF16)
        for s in range(STEP):
            at = i * STEP + s
            gate = gate_v[s]
            mixed = [fold(tn(prob_v[at, w], kv_v[at, w * WIN : w * WIN + KEYS, CH:])) for w in range(2)]
            attended = jnp.concatenate(mixed, axis=0)
            gated_v[s] = (attended * gate).astype(BF16)
            dgate_v[at] = (dgated_v[s].astype(F32) * attended * (gate * (1.0 - gate))).astype(BF16)

        out = x.astype(F32) + nn(gated_v[...].reshape(STEP * BLOCK, CH), wo_ref[...])
        upd_v[part] = out.astype(BF16).reshape(STEP, BLOCK, CH)

    def second_pass(i):
        part = pl.ds(i * STEP, STEP)
        for s in range(STEP):
            at = i * STEP + s
            dkv_v[s, :, :CH] = (nn(both(dscore_v[at, 0], dscore_v[at, 1]), expand(q_v[at])) * SCALE).astype(BF16)
            dkv_v[s, :, CH:] = nn(both(prob_v[at, 0], prob_v[at, 1]), expand(datt_v[at])).astype(BF16)

        glo = nt(dkv_v[:, :HALO].reshape(STEP * HALO, 2 * CH), wkv_ref[...])
        glo_v[part] = glo.astype(BF16).reshape(STEP, HALO, CH)
        ghi = nt(dkv_v[:, HALO + BLOCK :].reshape(STEP * HALO, 2 * CH), wkv_ref[...])
        ghi_v[part] = ghi.astype(BF16).reshape(STEP, HALO, CH)

        @pl.when(has_prev)
        def _():
            grad_to_prev(i).start()

        @pl.when(has_next)
        def _():
            grad_to_next(i).start()

        for s in range(STEP):
            at = i * STEP + s
            for w in range(2):
                dq = fold(tn(dscore_v[at, w], kv_v[at, w * WIN : w * WIN + KEYS, :CH]))
                dq_v[s, w * WIN : (w + 1) * WIN] = (dq * SCALE).astype(BF16)
        dquery = dq_v[...].reshape(STEP * BLOCK, CH)
        dgate = dgate_v[part].reshape(STEP * BLOCK, CH)
        own = nt(dkv_v[:, HALO : HALO + BLOCK].reshape(STEP * BLOCK, 2 * CH), wkv_ref[...])
        own = own + nt(jnp.concatenate([dquery, dgate], axis=1), wqg_ref[...])
        own = own + dy_v[part].reshape(STEP * BLOCK, CH).astype(F32)
        center_v[part] = own.reshape(STEP, BLOCK, CH)

        @pl.when(i >= LAG)
        def _():
            finish(i - LAG)

    def a_copy(peer, slot):
        return pltpu.make_async_remote_copy(
            src_ref=part_a, dst_ref=red_a.at[slot],
            send_sem=a_send.at[peer], recv_sem=a_recv.at[slot],
            device_id=(row, peer), device_id_type=MESH)

    def b_copy(peer, slot):
        return pltpu.make_async_remote_copy(
            src_ref=part_b, dst_ref=red_b.at[slot],
            send_sem=b_send.at[peer], recv_sem=b_recv.at[slot],
            device_id=(peer, col), device_id_type=MESH)

    @pl.loop(0, chunks)
    def _(i):
        first_pass(i)

        @pl.when(i >= DELAY)
        def _():
            second_pass(i - DELAY)

    gap32 = jnp.zeros((WIN, KEYS), F32)
    dbias = jnp.concatenate(
        [jnp.concatenate([dbt_v[0], gap32], axis=0), jnp.concatenate([gap32, dbt_v[1]], axis=0)], axis=1)
    dtable = tn(key_hot32, dbias, HI)[: 3 * TOK]
    by_token = jnp.concatenate(
        [
            jnp.where(query_token == t, dtable[s * TOK : (s + 1) * TOK], 0.0)
            for s in range(3) for t in range(TOK)
        ], axis=0)
    head_row = (iota((8, LANES), 1) % KEYS) // WIN
    to_head = (head_row == iota((8, LANES), 0)).astype(F32)
    dbias_rows = nt(to_head, by_token, HI).astype(BF16).astype(F32)
    normed, rstd = band_normed()
    part_a[...] = nn(dbias_rows, normed, HI)
    red_a[col] = part_a[...]

    @pl.loop(1, cols)
    def _(d):
        a_copy(lax.rem(col + d, cols), col).start()

    weight = jnp.concatenate([pwt_v[...], jnp.zeros((8 - HEADS, CH), F32)], axis=0)
    dnormed = tn(dbias_rows, weight, HI)
    dvalues = rstd * (
        dnormed - jnp.mean(dnormed, axis=1, keepdims=True)
        - normed * jnp.mean(dnormed * normed, axis=1, keepdims=True))
    for s in range(3):
        for t in range(TOK):
            at = (s * TOK + t) * TOK
            bandgrad_v[t, s * TOK : (s + 1) * TOK] = dvalues[at : at + TOK].astype(BF16)

    def send_piece(cond, target, d, wide, first):
        @pl.when(jnp.logical_and(cond, target != col))
        def _():
            piece_copy(target, d, wide, first).start()

        @pl.when(jnp.logical_and(cond, target == col))
        def _():
            piece_v[d + 1] = bandgrad_v[...]

    to_owners(send_piece)

    @pl.loop(chunks - DELAY, chunks - DELAY + HALF)
    def _(i):
        second_pass(i)

    @pl.loop(1, cols)
    def _(d):
        source = lax.rem(col + d, cols)
        a_copy(source, source).wait_recv()

    total = red_a[0]
    for j in range(1, cols):
        total = total + red_a[j]
    part_b[...] = total
    red_b[row] = total

    @pl.loop(1, rows)
    def _(d):
        b_copy(lax.rem(row + d, rows), row).start()

    @pl.loop(chunks - DELAY + HALF, chunks)
    def _(i):
        second_pass(i)

    def place(d, wide, first):
        j = delta + d

        @pl.when(jnp.logical_and(inside(j), j != col))
        def _():
            piece_copy(clamped(j), d, wide, first).wait_recv()

        @pl.when(inside(j))
        def _():
            for s in range(first, first + wide):
                at = pl.ds(pl.multiple_of((d + s - 1) * TOK, TOK), TOK)
                for t in range(TOK):
                    pair_out[clamped(j) * TOK + t, at] = piece_v[d + 1, t, s * TOK : (s + 1) * TOK]

    all_readers(place)

    @pl.loop(chunks - LAG, chunks)
    def _(i):
        finish(i)

    def sent_piece(cond, target, d, wide, first):
        @pl.when(jnp.logical_and(cond, target != col))
        def _():
            piece_copy(target, d, wide, first).wait_send()

    to_owners(sent_piece)
    all_readers(band_sent)

    @pl.loop(0, chunks)
    def _(i):
        @pl.when(has_next)
        def _():
            to_next(i).wait_send()
            grad_to_next(i).wait_send()

        @pl.when(has_prev)
        def _():
            to_prev(i).wait_send()
            grad_to_prev(i).wait_send()

    @pl.loop(1, cols)
    def _(d):
        a_copy(lax.rem(col + d, cols), col).wait_send()

    @pl.loop(1, rows)
    def _(d):
        source = lax.rem(row + d, rows)
        b_copy(source, source).wait_recv()

    total = red_b[0]
    for j in range(1, rows):
        total = total + red_b[j]
    wgrad_out[...] = total

    @pl.loop(1, rows)
    def _(d):
        b_copy(lax.rem(row + d, rows), row).wait_send()


def final_kernel(upd_in, grad_in, pair_in, wsum, upd_out, grad_out, pair_out, wgrad, sems):
    copies = [
        pltpu.make_async_copy(src, dst, sems.at[n])
        for n, (src, dst) in enumerate([(pair_in, pair_out), (upd_in, upd_out), (grad_in, grad_out)])
    ]
    for copy in copies:
        copy.start()
    wgrad[...] = wsum[:HEADS]
    for copy in copies:
        copy.wait()


def on_device(rows, cols, atom_rows, pair_rep, wqg, wkv, wo, pw, counts, token_mask, cotangent):
    samples = atom_rows.shape[0]
    chunks = samples // STEP
    vmem = pl.BlockSpec(memory_space=pltpu.VMEM)
    hbm = pl.BlockSpec(memory_space=pltpu.HBM)
    own = (samples, BLOCK, CH)
    halo = (samples, HALO, CH)
    dma = pltpu.SemaphoreType.DMA
    upd, grad, pair, wsum = pl.pallas_call(
        functools.partial(main_kernel, rows, cols, samples),
        out_shape=(
            jax.ShapeDtypeStruct(own, BF16),
            jax.ShapeDtypeStruct(own, BF16),
            jax.ShapeDtypeStruct(pair_rep.shape, BF16),
            jax.ShapeDtypeStruct((8, CH), F32),
        ),
        in_specs=[hbm] * 9,
        out_specs=(vmem,) * 4,
        scratch_shapes=[
            pltpu.SMEM((TOK, rows * cols), jnp.int32), pltpu.SMEM((rows * cols * TOK,), jnp.int32),
            pltpu.VMEM((CH, 2 * CH), BF16), pltpu.VMEM((CH, 2 * CH), BF16), pltpu.VMEM((CH, CH), BF16),
            pltpu.VMEM((HEADS, CH), F32), pltpu.VMEM((CH, 8), F32),
            pltpu.VMEM(own, BF16), pltpu.VMEM(own, BF16),
            pltpu.VMEM(halo, BF16), pltpu.VMEM(halo, BF16),
            pltpu.VMEM(halo, BF16), pltpu.VMEM(halo, BF16),
            pltpu.VMEM(halo, BF16), pltpu.VMEM(halo, BF16),
            pltpu.VMEM(own, F32),
            pltpu.VMEM((TOK, 3 * TOK, CH), BF16), pltpu.VMEM((TOK, 3 * TOK, CH), BF16),
            pltpu.VMEM((rows + 2, TOK, 3 * TOK, CH), BF16),
            pltpu.VMEM((2, KEYS, KEYS), F32), pltpu.VMEM((2, KEYS, KEYS), F32),
            pltpu.VMEM((samples, EXT, 2 * CH), BF16), pltpu.VMEM((STEP, EXT, 2 * CH), BF16),
            pltpu.VMEM(own, BF16), pltpu.VMEM((STEP, BLOCK, CH), F32),
            pltpu.VMEM((STEP, BLOCK, CH), BF16), pltpu.VMEM((STEP, BLOCK, CH), BF16),
            pltpu.VMEM(own, BF16), pltpu.VMEM((STEP, BLOCK, CH), BF16), pltpu.VMEM(own, BF16),
            pltpu.VMEM((samples, 2, KEYS, KEYS), BF16), pltpu.VMEM((samples, 2, KEYS, KEYS), BF16),
            pltpu.VMEM((STEP, EXT, LANES), F32), pltpu.VMEM((STEP, EXT, LANES), F32),
            pltpu.VMEM((cols, 8, CH), F32), pltpu.VMEM((rows, 8, CH), F32),
            pltpu.VMEM((8, CH), F32), pltpu.VMEM((8, CH), F32),
            dma((8,)),
            dma((chunks,)), dma((chunks,)), dma((chunks,)), dma((chunks,)),
            dma((chunks,)), dma((chunks,)), dma((chunks,)), dma((chunks,)),
            dma((rows + 2,)), dma((2,)), dma((2,)), dma((rows + 2,)),
            dma((cols,)), dma((cols,)), dma((rows,)), dma((rows,)),
        ],
        compiler_params=pltpu.CompilerParams(
            collective_id=0, has_side_effects=True, vmem_limit_bytes=40 * 2**20),
    )(*[
        pltpu.with_memory_space_constraint(array, pltpu.HBM)
        for array in (counts.T, token_mask, atom_rows, pair_rep, wqg, wkv, wo, pw.T, cotangent)
    ])
    upd, grad, pair_grad, wgrad = pl.pallas_call(
        final_kernel,
        out_shape=(
            jax.ShapeDtypeStruct(own, BF16),
            jax.ShapeDtypeStruct(own, BF16),
            jax.ShapeDtypeStruct(pair_rep.shape, BF16),
            jax.ShapeDtypeStruct((HEADS, CH), F32),
        ),
        in_specs=[vmem, vmem, vmem, vmem],
        out_specs=(hbm, hbm, hbm, vmem),
        scratch_shapes=[dma((3,))],
        compiler_params=pltpu.CompilerParams(vmem_limit_bytes=8 * 2**20),
    )(upd, grad, pair, wsum)
    return upd, grad, pair_grad, wgrad.T


def solution(mesh):
    rows, cols = mesh.shape["row"], mesh.shape["col"]
    atoms = P(None, ("row", "col"), None)
    pairs = P("row", "col", None)
    return jax.shard_map(
        functools.partial(on_device, rows, cols),
        mesh=mesh,
        in_specs=(atoms, pairs, P(), P(), P(), P(), P(), P(), atoms),
        out_specs=(atoms, atoms, pairs, P()),
        check_vma=False,
    )
```

```python
import functools
import math

import jax
import jax.numpy as jnp
from jax import lax
from jax.experimental import pallas as pl
from jax.experimental.pallas import tpu as pltpu
from jax.sharding import PartitionSpec as P

BLOCK = 64
TOK = 8
HEADS = 4
WIN = 32
KEYS = 128
HALO = 48
CH = 128
EXT = BLOCK + 2 * HALO
LANES = 2 * HEADS * WIN
EPS = 1e-05
MASKED = -1000000000.0
SCALE = 1.0 / math.sqrt(CH // HEADS)
STEP = 8
AHEAD = 3
LAG = 2
DELAY = 1
HALF = 1

F32 = jnp.float32
BF16 = jnp.bfloat16
HI = lax.Precision.HIGHEST
MESH = pl.DeviceIdType.MESH


def nn(a, b, precision=None):
    return lax.dot_general(a, b, (((1,), (0,)), ((), ())), precision=precision, preferred_element_type=F32)


def nt(a, b, precision=None):
    return lax.dot_general(a, b, (((1,), (1,)), ((), ())), precision=precision, preferred_element_type=F32)


def tn(a, b, precision=None):
    return lax.dot_general(a, b, (((0,), (0,)), ((), ())), precision=precision, preferred_element_type=F32)


def iota(shape, dim):
    return lax.broadcasted_iota(jnp.int32, shape, dim)


def normalize(values):
    centered = values - jnp.mean(values, axis=1, keepdims=True)
    rstd = lax.rsqrt(jnp.mean(centered * centered, axis=1, keepdims=True) + EPS)
    return centered * rstd, rstd


def totals_of(counts, group):
    running, total = [], 0
    for j in range(TOK):
        total = total + counts[j, group]
        running.append(total)
    return running


def main_kernel(
    rows, cols, samples,
    counts_hbm, mask_hbm, x_hbm, pair_hbm, wqg_hbm, wkv_hbm, wo_hbm, pw_hbm, dy_hbm,
    upd_v, grad_v, pair_out, wgrad_out,
    counts, mask, wqg_ref, wkv_ref, wo_ref, pwt_v, pw_v,
    x_v, dy_v, lo_v, hi_v, glo_v, ghi_v, gprev_v, gnext_v, center_v,
    band_v, bandgrad_v, piece_v, bt_v, dbt_v, kv_v, dkv_v, q_v, gate_v, dgated_v, gated_v, dgate_v, dq_v,
    datt_v, prob_v, dscore_v, logit_v, dprob_v,
    red_a, red_b, part_a, part_b,
    in_sem, lo_send, hi_send, lo_recv, hi_recv, glo_send, ghi_send, gp_recv, gn_recv,
    band_send, band_recv, piece_send, piece_recv, a_send, a_recv, b_send, b_recv,
):
    chunks = samples // STEP
    blocks = rows * cols
    row = lax.axis_index("row")
    col = lax.axis_index("col")
    me = row * cols + col
    has_prev = me > 0
    has_next = me < blocks - 1
    before = jnp.maximum(me - 1, 0)
    after = jnp.minimum(me + 1, blocks - 1)
    prev_id = (before // cols, before % cols)
    next_id = (after // cols, after % cols)

    barrier = pltpu.get_barrier_semaphore()

    @pl.loop(1, cols)
    def _(d):
        pl.semaphore_signal(barrier, inc=1, device_id=(row, lax.rem(col + d, cols)), device_id_type=MESH)

    @pl.loop(1, rows)
    def _(d):
        pl.semaphore_signal(barrier, inc=1, device_id=(lax.rem(row + d, rows), col), device_id_type=MESH)

    far_next = jnp.logical_and(col == cols - 1, has_next)
    far_prev = jnp.logical_and(col == 0, has_prev)

    @pl.when(far_next)
    def _():
        pl.semaphore_signal(barrier, inc=1, device_id=next_id, device_id_type=MESH)

    @pl.when(far_prev)
    def _():
        pl.semaphore_signal(barrier, inc=1, device_id=prev_id, device_id_type=MESH)

    small_in = [
        pltpu.make_async_copy(src, dst, in_sem.at[n])
        for n, (src, dst) in enumerate([(counts_hbm, counts), (mask_hbm, mask), (pw_hbm, pwt_v)])
    ]
    large_in = [
        pltpu.make_async_copy(src, dst, in_sem.at[3 + n])
        for n, (src, dst) in enumerate(
            [(wkv_hbm, wkv_ref), (wqg_hbm, wqg_ref), (wo_hbm, wo_ref), (x_hbm, x_v), (dy_hbm, dy_v)])
    ]
    for copy in small_in + large_in:
        copy.start()

    @pl.when(jnp.logical_not(has_prev))
    def _():
        lo_v[...] = jnp.zeros_like(lo_v)
        gprev_v[...] = jnp.zeros_like(gprev_v)
        band_v[:, :TOK] = jnp.zeros((TOK, TOK, CH), BF16)

    @pl.when(jnp.logical_not(has_next))
    def _():
        hi_v[...] = jnp.zeros_like(hi_v)
        gnext_v[...] = jnp.zeros_like(gnext_v)
        band_v[:, 2 * TOK :] = jnp.zeros((TOK, TOK, CH), BF16)

    for copy in small_in:
        copy.wait()

    g_prev = jnp.maximum(me - 1, 0)
    g_next = jnp.minimum(me + 1, blocks - 1)
    run_prev, run_own, run_next = totals_of(counts, g_prev), totals_of(counts, me), totals_of(counts, g_next)
    atom = iota((EXT, 32), 0)
    is_lo, is_hi = atom < HALO, atom >= HALO + BLOCK
    local = jnp.where(is_lo, atom + (BLOCK - HALO), jnp.where(is_hi, atom - (HALO + BLOCK), atom - HALO))
    token = jnp.where(is_lo, 0, jnp.where(is_hi, 2 * TOK, TOK))
    for j in range(TOK):
        limit = jnp.where(is_lo, run_prev[j], jnp.where(is_hi, run_next[j], run_own[j]))
        token = token + (limit <= local).astype(jnp.int32)
    key_hot32 = (token == iota((EXT, 32), 1)).astype(F32)
    key_hot = key_hot32.astype(BF16)

    lane = iota((TOK, LANES), 1)
    query = (lane // KEYS) * WIN + lane % WIN
    query_token = jnp.zeros((TOK, LANES), jnp.int32)
    for j in range(TOK):
        query_token = query_token + (run_own[j] <= query).astype(jnp.int32)

    slot_row = iota((32, LANES), 0)
    mask_rows = jnp.zeros((32, LANES), F32)
    for u in range(3 * TOK):
        where_to = me * TOK + u - TOK
        bit = mask[jnp.clip(where_to, 0, blocks * TOK - 1)]
        bit = jnp.where(jnp.logical_and(where_to >= 0, where_to < blocks * TOK), bit, 0)
        mask_rows = jnp.where(slot_row == u, bit.astype(F32), mask_rows)
    valid = nn(key_hot, mask_rows.astype(BF16))

    pl.semaphore_wait(
        barrier, (cols - 1) + (rows - 1) + far_next.astype(jnp.int32) + far_prev.astype(jnp.int32)
    )

    def to_next(i):
        return pltpu.make_async_remote_copy(
            src_ref=x_hbm.at[pl.ds(i * STEP, STEP), pl.ds(BLOCK - HALO, HALO)],
            dst_ref=lo_v.at[pl.ds(i * STEP, STEP)],
            send_sem=lo_send.at[i], recv_sem=lo_recv.at[i],
            device_id=next_id, device_id_type=MESH)

    def to_prev(i):
        return pltpu.make_async_remote_copy(
            src_ref=x_hbm.at[pl.ds(i * STEP, STEP), pl.ds(0, HALO)],
            dst_ref=hi_v.at[pl.ds(i * STEP, STEP)],
            send_sem=hi_send.at[i], recv_sem=hi_recv.at[i],
            device_id=prev_id, device_id_type=MESH)

    def grad_to_prev(i):
        return pltpu.make_async_remote_copy(
            src_ref=glo_v.at[pl.ds(i * STEP, STEP)],
            dst_ref=gnext_v.at[pl.ds(i * STEP, STEP)],
            send_sem=glo_send.at[i], recv_sem=gn_recv.at[i],
            device_id=prev_id, device_id_type=MESH)

    def grad_to_next(i):
        return pltpu.make_async_remote_copy(
            src_ref=ghi_v.at[pl.ds(i * STEP, STEP)],
            dst_ref=gprev_v.at[pl.ds(i * STEP, STEP)],
            send_sem=ghi_send.at[i], recv_sem=gp_recv.at[i],
            device_id=next_id, device_id_type=MESH)

    delta = rows * col - cols * row

    def inside(j):
        return jnp.logical_and(j >= 0, j < cols)

    def clamped(j):
        return jnp.clip(j, 0, cols - 1)

    def band_refs(d, j, wide, first):
        k = d - 1 + first
        return (
            pair_hbm.at[pl.ds(j * TOK, TOK), pl.ds(pl.multiple_of(k * TOK, TOK), wide * TOK)],
            band_v.at[:, pl.ds(first * TOK, wide * TOK)])

    def band_copy(d, j, wide, first):
        src, dst = band_refs(d, j, wide, first)
        return pltpu.make_async_remote_copy(
            src_ref=src, dst_ref=dst,
            send_sem=band_send.at[d + 1], recv_sem=band_recv.at[0 if wide > 1 else 1],
            device_id=(row, j), device_id_type=MESH)

    def band_local(d, j, wide, first):
        src, dst = band_refs(d, j, wide, first)
        return pltpu.make_async_copy(src, dst, band_send.at[d + 1])

    def send_band(d, wide, first):
        j = delta + d

        @pl.when(jnp.logical_and(inside(j), j != col))
        def _():
            band_copy(d, clamped(j), wide, first).start()

        @pl.when(jnp.logical_and(inside(j), j == col))
        def _():
            band_local(d, clamped(j), wide, first).start()

    def band_sent(d, wide, first):
        j = delta + d

        @pl.when(jnp.logical_and(inside(j), j != col))
        def _():
            band_copy(d, clamped(j), wide, first).wait_send()

    def all_readers(act):
        @pl.loop(1, rows - 1)
        def _(d):
            act(d, 3, 0)

        act(0, 2, 1)
        act(rows - 1, 2, 0)
        act(-1, 1, 2)
        act(rows, 1, 0)

    owner = me // rows
    mine = me % rows
    side_low = jnp.logical_and(mine == 0, has_prev)
    side_high = jnp.logical_and(mine == rows - 1, has_next)

    def receive_band(cond, source, d, wide, first):
        @pl.when(jnp.logical_and(cond, source != col))
        def _():
            band_copy(d, col, wide, first).wait_recv()

        @pl.when(jnp.logical_and(cond, source == col))
        def _():
            band_local(d, col, wide, first).wait()

    def piece_copy(target, d, wide, first):
        at = pl.ds(first * TOK, wide * TOK)
        return pltpu.make_async_remote_copy(
            src_ref=bandgrad_v.at[:, at], dst_ref=piece_v.at[d + 1, :, at],
            send_sem=piece_send.at[0 if wide > 1 else 1], recv_sem=piece_recv.at[d + 1],
            device_id=(row, target), device_id_type=MESH)

    def to_owners(act):
        act(jnp.logical_and(mine > 0, mine < rows - 1), owner, mine, 3, 0)
        act(mine == 0, owner, 0, 2, 1)
        act(mine == rows - 1, owner, rows - 1, 2, 0)
        act(side_high, owner + 1, -1, 1, 2)
        act(side_low, owner - 1, rows, 1, 0)

    def send_rows(i):
        @pl.when(has_next)
        def _():
            to_next(i).start()

        @pl.when(has_prev)
        def _():
            to_prev(i).start()

    send_rows(0)
    all_readers(send_band)

    @pl.loop(1, AHEAD)
    def _(i):
        send_rows(i)

    to_owners(receive_band)

    def band_normed():
        return normalize(
            jnp.concatenate(
                [band_v[t, s * TOK : (s + 1) * TOK].astype(F32) for s in range(3) for t in range(TOK)], axis=0))

    pw_v[...] = jnp.concatenate([pwt_v[...], jnp.zeros((8 - HEADS, CH), F32)], axis=0).T
    head_lane = (iota((CH, LANES), 1) % KEYS) // WIN
    spread_weight = jnp.zeros((CH, LANES), F32)
    for h in range(HEADS):
        spread_weight = jnp.where(head_lane == h, pw_v[:, h : h + 1], spread_weight)
    normed, _ = band_normed()
    projected = nn(normed, spread_weight, HI)
    table = []
    for s in range(3):
        part = jnp.zeros((TOK, LANES), F32)
        for t in range(TOK):
            at = (s * TOK + t) * TOK
            part = jnp.where(query_token == t, projected[at : at + TOK], part)
        table.append(part)
    table = jnp.concatenate(table, axis=0)
    table = jnp.concatenate([table, jnp.zeros((8, LANES), F32)], axis=0).astype(BF16)
    bias = jnp.where(valid > 0.5, nn(key_hot, table), nn(key_hot, table) + MASKED)
    for w in range(2):
        bt_v[w] = bias[w * WIN : w * WIN + KEYS, w * KEYS : (w + 1) * KEYS]
    dbt_v[...] = jnp.zeros_like(dbt_v)
    pair_out[...] = jnp.zeros_like(pair_out)

    head_of = iota((WIN, CH), 1) // WIN
    head_mask = [(head_of == h).astype(BF16) for h in range(HEADS)]

    def expand(a):
        return jnp.concatenate(
            [a[w * WIN : (w + 1) * WIN] * head_mask[h] for w in range(2) for h in range(HEADS)], axis=0)

    def fold(a):
        out = a[:WIN]
        for h in range(1, HEADS):
            out = jnp.where(head_of == h, a[h * WIN : (h + 1) * WIN], out)
        return out

    gap = jnp.zeros((WIN, KEYS), BF16)

    def both(a0, a1):
        return jnp.concatenate(
            [jnp.concatenate([a0, gap], axis=0), jnp.concatenate([gap, a1], axis=0)], axis=1)

    for copy in large_in:
        copy.wait()

    def finish(i):
        @pl.when(has_next)
        def _():
            grad_to_prev(i).wait_recv()

        @pl.when(has_prev)
        def _():
            grad_to_next(i).wait_recv()

        part = pl.ds(i * STEP, STEP)
        from_prev = gprev_v[part].astype(F32)
        from_next = gnext_v[part].astype(F32)
        cut = BLOCK - HALO
        grad_v[part, 0:cut] = (center_v[part, 0:cut] + from_prev[:, :cut]).astype(BF16)
        grad_v[part, cut:HALO] = (
            center_v[part, cut:HALO] + from_prev[:, cut:] + from_next[:, : HALO - cut]).astype(BF16)
        grad_v[part, HALO:BLOCK] = (center_v[part, HALO:BLOCK] + from_next[:, HALO - cut :]).astype(BF16)

    def first_pass(i):
        @pl.when(i + AHEAD < chunks)
        def _():
            send_rows(i + AHEAD)

        part = pl.ds(i * STEP, STEP)
        x3 = x_v[part]
        x = x3.reshape(STEP * BLOCK, CH)
        dy = dy_v[part].reshape(STEP * BLOCK, CH)
        query_gate = nn(x, wqg_ref[...])
        q_v[part] = query_gate[:, :CH].astype(BF16).reshape(STEP, BLOCK, CH)
        gate_v[...] = jax.nn.sigmoid(query_gate[:, CH:]).reshape(STEP, BLOCK, CH)
        dgated_v[...] = nt(dy, wo_ref[...]).astype(BF16).reshape(STEP, BLOCK, CH)
        kv_v[part, HALO : HALO + BLOCK] = nn(x, wkv_ref[...]).astype(BF16).reshape(STEP, BLOCK, 2 * CH)

        @pl.when(has_prev)
        def _():
            to_next(i).wait_recv()

        @pl.when(has_next)
        def _():
            to_prev(i).wait_recv()

        lo = lo_v[part].reshape(STEP * HALO, CH)
        hi = hi_v[part].reshape(STEP * HALO, CH)
        kv_v[part, :HALO] = nn(lo, wkv_ref[...]).astype(BF16).reshape(STEP, HALO, 2 * CH)
        kv_v[part, HALO + BLOCK :] = nn(hi, wkv_ref[...]).astype(BF16).reshape(STEP, HALO, 2 * CH)

        for s in range(STEP):
            at = i * STEP + s
            datt = (dgated_v[s].astype(F32) * gate_v[s]).astype(BF16)
            datt_v[at] = datt
            logit_v[s] = nt(kv_v[at, :, :CH], expand(q_v[at]))
            dprob_v[s] = nt(kv_v[at, :, CH:], expand(datt))
        for w in range(2):
            ks = slice(w * WIN, w * WIN + KEYS)
            ls = slice(w * KEYS, (w + 1) * KEYS)
            for s in range(STEP):
                at = i * STEP + s
                score = logit_v[s, ks, ls] * SCALE + bt_v[w]
                e = jnp.exp(score - jnp.max(score, axis=0, keepdims=True))
                p = e * (1.0 / jnp.sum(e, axis=0, keepdims=True))
                t = dprob_v[s, ks, ls] * p
                ds = t - p * jnp.sum(t, axis=0, keepdims=True)
                dbt_v[w] += ds
                prob_v[at, w] = p.astype(BF16)
                dscore_v[at, w] = ds.astype(BF16)
        for s in range(STEP):
            at = i * STEP + s
            gate = gate_v[s]
            mixed = [fold(tn(prob_v[at, w], kv_v[at, w * WIN : w * WIN + KEYS, CH:])) for w in range(2)]
            attended = jnp.concatenate(mixed, axis=0)
            gated_v[s] = (attended * gate).astype(BF16)
            dgate_v[at] = (dgated_v[s].astype(F32) * attended * (gate * (1.0 - gate))).astype(BF16)

        out = x.astype(F32) + nn(gated_v[...].reshape(STEP * BLOCK, CH), wo_ref[...])
        upd_v[part] = out.astype(BF16).reshape(STEP, BLOCK, CH)

    def second_pass(i):
        part = pl.ds(i * STEP, STEP)
        for s in range(STEP):
            at = i * STEP + s
            dkv_v[s, :, :CH] = (nn(both(dscore_v[at, 0], dscore_v[at, 1]), expand(q_v[at])) * SCALE).astype(BF16)
            dkv_v[s, :, CH:] = nn(both(prob_v[at, 0], prob_v[at, 1]), expand(datt_v[at])).astype(BF16)

        glo = nt(dkv_v[:, :HALO].reshape(STEP * HALO, 2 * CH), wkv_ref[...])
        glo_v[part] = glo.astype(BF16).reshape(STEP, HALO, CH)
        ghi = nt(dkv_v[:, HALO + BLOCK :].reshape(STEP * HALO, 2 * CH), wkv_ref[...])
        ghi_v[part] = ghi.astype(BF16).reshape(STEP, HALO, CH)

        @pl.when(has_prev)
        def _():
            grad_to_prev(i).start()

        @pl.when(has_next)
        def _():
            grad_to_next(i).start()

        for s in range(STEP):
            at = i * STEP + s
            for w in range(2):
                dq = fold(tn(dscore_v[at, w], kv_v[at, w * WIN : w * WIN + KEYS, :CH]))
                dq_v[s, w * WIN : (w + 1) * WIN] = (dq * SCALE).astype(BF16)
        dquery = dq_v[...].reshape(STEP * BLOCK, CH)
        dgate = dgate_v[part].reshape(STEP * BLOCK, CH)
        own = nt(dkv_v[:, HALO : HALO + BLOCK].reshape(STEP * BLOCK, 2 * CH), wkv_ref[...])
        own = own + nt(jnp.concatenate([dquery, dgate], axis=1), wqg_ref[...])
        own = own + dy_v[part].reshape(STEP * BLOCK, CH).astype(F32)
        center_v[part] = own.reshape(STEP, BLOCK, CH)

        @pl.when(i >= LAG)
        def _():
            finish(i - LAG)

    def a_copy(peer, slot):
        return pltpu.make_async_remote_copy(
            src_ref=part_a, dst_ref=red_a.at[slot],
            send_sem=a_send.at[peer], recv_sem=a_recv.at[slot],
            device_id=(row, peer), device_id_type=MESH)

    def b_copy(peer, slot):
        return pltpu.make_async_remote_copy(
            src_ref=part_b, dst_ref=red_b.at[slot],
            send_sem=b_send.at[peer], recv_sem=b_recv.at[slot],
            device_id=(peer, col), device_id_type=MESH)

    @pl.loop(0, chunks)
    def _(i):
        first_pass(i)

        @pl.when(i >= DELAY)
        def _():
            second_pass(i - DELAY)

    gap32 = jnp.zeros((WIN, KEYS), F32)
    dbias = jnp.concatenate(
        [jnp.concatenate([dbt_v[0], gap32], axis=0), jnp.concatenate([gap32, dbt_v[1]], axis=0)], axis=1)
    dtable = tn(key_hot32, dbias, HI)[: 3 * TOK]
    by_token = jnp.concatenate(
        [
            jnp.where(query_token == t, dtable[s * TOK : (s + 1) * TOK], 0.0)
            for s in range(3) for t in range(TOK)
        ], axis=0)
    head_row = (iota((8, LANES), 1) % KEYS) // WIN
    to_head = (head_row == iota((8, LANES), 0)).astype(F32)
    dbias_rows = nt(to_head, by_token, HI).astype(BF16).astype(F32)
    normed, rstd = band_normed()
    part_a[...] = nn(dbias_rows, normed, HI)
    red_a[col] = part_a[...]

    @pl.loop(1, cols)
    def _(d):
        a_copy(lax.rem(col + d, cols), col).start()

    weight = jnp.concatenate([pwt_v[...], jnp.zeros((8 - HEADS, CH), F32)], axis=0)
    dnormed = tn(dbias_rows, weight, HI)
    dvalues = rstd * (
        dnormed - jnp.mean(dnormed, axis=1, keepdims=True)
        - normed * jnp.mean(dnormed * normed, axis=1, keepdims=True))
    for s in range(3):
        for t in range(TOK):
            at = (s * TOK + t) * TOK
            bandgrad_v[t, s * TOK : (s + 1) * TOK] = dvalues[at : at + TOK].astype(BF16)

    def send_piece(cond, target, d, wide, first):
        @pl.when(jnp.logical_and(cond, target != col))
        def _():
            piece_copy(target, d, wide, first).start()

        @pl.when(jnp.logical_and(cond, target == col))
        def _():
            piece_v[d + 1] = bandgrad_v[...]

    to_owners(send_piece)

    @pl.loop(chunks - DELAY, chunks - DELAY + HALF)
    def _(i):
        second_pass(i)

    @pl.loop(1, cols)
    def _(d):
        source = lax.rem(col + d, cols)
        a_copy(source, source).wait_recv()

    total = red_a[0]
    for j in range(1, cols):
        total = total + red_a[j]
    part_b[...] = total
    red_b[row] = total

    @pl.loop(1, rows)
    def _(d):
        b_copy(lax.rem(row + d, rows), row).start()

    @pl.loop(chunks - DELAY + HALF, chunks)
    def _(i):
        second_pass(i)

    def place(d, wide, first):
        j = delta + d

        @pl.when(jnp.logical_and(inside(j), j != col))
        def _():
            piece_copy(clamped(j), d, wide, first).wait_recv()

        @pl.when(inside(j))
        def _():
            for s in range(first, first + wide):
                at = pl.ds(pl.multiple_of((d + s - 1) * TOK, TOK), TOK)
                for t in range(TOK):
                    pair_out[clamped(j) * TOK + t, at] = piece_v[d + 1, t, s * TOK : (s + 1) * TOK]

    all_readers(place)

    @pl.loop(chunks - LAG, chunks)
    def _(i):
        finish(i)

    def sent_piece(cond, target, d, wide, first):
        @pl.when(jnp.logical_and(cond, target != col))
        def _():
            piece_copy(target, d, wide, first).wait_send()

    to_owners(sent_piece)
    all_readers(band_sent)

    @pl.loop(0, chunks)
    def _(i):
        @pl.when(has_next)
        def _():
            to_next(i).wait_send()
            grad_to_next(i).wait_send()

        @pl.when(has_prev)
        def _():
            to_prev(i).wait_send()
            grad_to_prev(i).wait_send()

    @pl.loop(1, cols)
    def _(d):
        a_copy(lax.rem(col + d, cols), col).wait_send()

    @pl.loop(1, rows)
    def _(d):
        source = lax.rem(row + d, rows)
        b_copy(source, source).wait_recv()

    total = red_b[0]
    for j in range(1, rows):
        total = total + red_b[j]
    wgrad_out[...] = total

    @pl.loop(1, rows)
    def _(d):
        b_copy(lax.rem(row + d, rows), row).wait_send()


def final_kernel(upd_in, grad_in, pair_in, wsum, upd_out, grad_out, pair_out, wgrad, sems):
    copies = [
        pltpu.make_async_copy(src, dst, sems.at[n])
        for n, (src, dst) in enumerate([(pair_in, pair_out), (upd_in, upd_out), (grad_in, grad_out)])
    ]
    for copy in copies:
        copy.start()
    wgrad[...] = wsum[:HEADS]
    for copy in copies:
        copy.wait()


def on_device(rows, cols, atom_rows, pair_rep, wqg, wkv, wo, pw, counts, token_mask, cotangent):
    samples = atom_rows.shape[0]
    chunks = samples // STEP
    vmem = pl.BlockSpec(memory_space=pltpu.VMEM)
    hbm = pl.BlockSpec(memory_space=pltpu.HBM)
    own = (samples, BLOCK, CH)
    halo = (samples, HALO, CH)
    dma = pltpu.SemaphoreType.DMA
    upd, grad, pair, wsum = pl.pallas_call(
        functools.partial(main_kernel, rows, cols, samples),
        out_shape=(
            jax.ShapeDtypeStruct(own, BF16),
            jax.ShapeDtypeStruct(own, BF16),
            jax.ShapeDtypeStruct(pair_rep.shape, BF16),
            jax.ShapeDtypeStruct((8, CH), F32),
        ),
        in_specs=[hbm] * 9,
        out_specs=(vmem,) * 4,
        scratch_shapes=[
            pltpu.SMEM((TOK, rows * cols), jnp.int32), pltpu.SMEM((rows * cols * TOK,), jnp.int32),
            pltpu.VMEM((CH, 2 * CH), BF16), pltpu.VMEM((CH, 2 * CH), BF16), pltpu.VMEM((CH, CH), BF16),
            pltpu.VMEM((HEADS, CH), F32), pltpu.VMEM((CH, 8), F32),
            pltpu.VMEM(own, BF16), pltpu.VMEM(own, BF16),
            pltpu.VMEM(halo, BF16), pltpu.VMEM(halo, BF16),
            pltpu.VMEM(halo, BF16), pltpu.VMEM(halo, BF16),
            pltpu.VMEM(halo, BF16), pltpu.VMEM(halo, BF16),
            pltpu.VMEM(own, F32),
            pltpu.VMEM((TOK, 3 * TOK, CH), BF16), pltpu.VMEM((TOK, 3 * TOK, CH), BF16),
            pltpu.VMEM((rows + 2, TOK, 3 * TOK, CH), BF16),
            pltpu.VMEM((2, KEYS, KEYS), F32), pltpu.VMEM((2, KEYS, KEYS), F32),
            pltpu.VMEM((samples, EXT, 2 * CH), BF16), pltpu.VMEM((STEP, EXT, 2 * CH), BF16),
            pltpu.VMEM(own, BF16), pltpu.VMEM((STEP, BLOCK, CH), F32),
            pltpu.VMEM((STEP, BLOCK, CH), BF16), pltpu.VMEM((STEP, BLOCK, CH), BF16),
            pltpu.VMEM(own, BF16), pltpu.VMEM((STEP, BLOCK, CH), BF16), pltpu.VMEM(own, BF16),
            pltpu.VMEM((samples, 2, KEYS, KEYS), BF16), pltpu.VMEM((samples, 2, KEYS, KEYS), BF16),
            pltpu.VMEM((STEP, EXT, LANES), F32), pltpu.VMEM((STEP, EXT, LANES), F32),
            pltpu.VMEM((cols, 8, CH), F32), pltpu.VMEM((rows, 8, CH), F32),
            pltpu.VMEM((8, CH), F32), pltpu.VMEM((8, CH), F32),
            dma((8,)),
            dma((chunks,)), dma((chunks,)), dma((chunks,)), dma((chunks,)),
            dma((chunks,)), dma((chunks,)), dma((chunks,)), dma((chunks,)),
            dma((rows + 2,)), dma((2,)), dma((2,)), dma((rows + 2,)),
            dma((cols,)), dma((cols,)), dma((rows,)), dma((rows,)),
        ],
        compiler_params=pltpu.CompilerParams(
            collective_id=0, has_side_effects=True, vmem_limit_bytes=40 * 2**20),
    )(*[
        pltpu.with_memory_space_constraint(array, pltpu.HBM)
        for array in (counts.T, token_mask, atom_rows, pair_rep, wqg, wkv, wo, pw.T, cotangent)
    ])
    upd, grad, pair_grad, wgrad = pl.pallas_call(
        final_kernel,
        out_shape=(
            jax.ShapeDtypeStruct(own, BF16),
            jax.ShapeDtypeStruct(own, BF16),
            jax.ShapeDtypeStruct(pair_rep.shape, BF16),
            jax.ShapeDtypeStruct((HEADS, CH), F32),
        ),
        in_specs=[vmem, vmem, vmem, vmem],
        out_specs=(hbm, hbm, hbm, vmem),
        scratch_shapes=[dma((3,))],
        compiler_params=pltpu.CompilerParams(vmem_limit_bytes=8 * 2**20),
    )(upd, grad, pair, wsum)
    return upd, grad, pair_grad, wgrad.T


def solution(mesh):
    rows, cols = mesh.shape["row"], mesh.shape["col"]
    atoms = P(None, ("row", "col"), None)
    pairs = P("row", "col", None)
    return jax.shard_map(
        functools.partial(on_device, rows, cols),
        mesh=mesh,
        in_specs=(atoms, pairs, P(), P(), P(), P(), P(), P(), atoms),
        out_specs=(atoms, atoms, pairs, P()),
        check_vma=False,
    )
```

```python
import functools
import math

import jax
import jax.numpy as jnp
from jax import lax
from jax.experimental import pallas as pl
from jax.experimental.pallas import tpu as pltpu
from jax.sharding import PartitionSpec as P

BLOCK = 64
TOK = 8
HEADS = 4
WIN = 32
KEYS = 128
HALO = 48
CH = 128
EXT = BLOCK + 2 * HALO
LANES = 2 * HEADS * WIN
EPS = 1e-05
MASKED = -1000000000.0
SCALE = 1.0 / math.sqrt(CH // HEADS)
STEP = 8
AHEAD = 3
LAG = 4
DELAY = 1
HALF = 1

F32 = jnp.float32
BF16 = jnp.bfloat16
HI = lax.Precision.HIGHEST
MESH = pl.DeviceIdType.MESH


def nn(a, b, precision=None):
    return lax.dot_general(a, b, (((1,), (0,)), ((), ())), precision=precision, preferred_element_type=F32)


def nt(a, b, precision=None):
    return lax.dot_general(a, b, (((1,), (1,)), ((), ())), precision=precision, preferred_element_type=F32)


def tn(a, b, precision=None):
    return lax.dot_general(a, b, (((0,), (0,)), ((), ())), precision=precision, preferred_element_type=F32)


def iota(shape, dim):
    return lax.broadcasted_iota(jnp.int32, shape, dim)


def normalize(values):
    centered = values - jnp.mean(values, axis=1, keepdims=True)
    rstd = lax.rsqrt(jnp.mean(centered * centered, axis=1, keepdims=True) + EPS)
    return centered * rstd, rstd


def totals_of(counts, group):
    running, total = [], 0
    for j in range(TOK):
        total = total + counts[j, group]
        running.append(total)
    return running


def main_kernel(
    rows, cols, samples,
    counts_hbm, mask_hbm, x_hbm, pair_hbm, wqg_hbm, wkv_hbm, wo_hbm, pw_hbm, dy_hbm,
    upd_v, grad_v, pair_out, wgrad_out,
    counts, mask, wqg_ref, wkv_ref, wo_ref, pwt_v, pw_v,
    x_v, dy_v, lo_v, hi_v, glo_v, ghi_v, gprev_v, gnext_v, center_v,
    band_v, bandgrad_v, piece_v, bt_v, dbt_v, kv_v, dkv_v, q_v, gate_v, dgated_v, gated_v, dgate_v, dq_v,
    datt_v, prob_v, dscore_v, logit_v, dprob_v,
    red_a, red_b, part_a, part_b,
    in_sem, lo_send, hi_send, lo_recv, hi_recv, glo_send, ghi_send, gp_recv, gn_recv,
    band_send, band_recv, piece_send, piece_recv, a_send, a_recv, b_send, b_recv,
):
    chunks = samples // STEP
    blocks = rows * cols
    row = lax.axis_index("row")
    col = lax.axis_index("col")
    me = row * cols + col
    has_prev = me > 0
    has_next = me < blocks - 1
    before = jnp.maximum(me - 1, 0)
    after = jnp.minimum(me + 1, blocks - 1)
    prev_id = (before // cols, before % cols)
    next_id = (after // cols, after % cols)

    barrier = pltpu.get_barrier_semaphore()

    @pl.loop(1, cols)
    def _(d):
        pl.semaphore_signal(barrier, inc=1, device_id=(row, lax.rem(col + d, cols)), device_id_type=MESH)

    @pl.loop(1, rows)
    def _(d):
        pl.semaphore_signal(barrier, inc=1, device_id=(lax.rem(row + d, rows), col), device_id_type=MESH)

    far_next = jnp.logical_and(col == cols - 1, has_next)
    far_prev = jnp.logical_and(col == 0, has_prev)

    @pl.when(far_next)
    def _():
        pl.semaphore_signal(barrier, inc=1, device_id=next_id, device_id_type=MESH)

    @pl.when(far_prev)
    def _():
        pl.semaphore_signal(barrier, inc=1, device_id=prev_id, device_id_type=MESH)

    small_in = [
        pltpu.make_async_copy(src, dst, in_sem.at[n])
        for n, (src, dst) in enumerate([(counts_hbm, counts), (mask_hbm, mask), (pw_hbm, pwt_v)])
    ]
    large_in = [
        pltpu.make_async_copy(src, dst, in_sem.at[3 + n])
        for n, (src, dst) in enumerate(
            [(wkv_hbm, wkv_ref), (wqg_hbm, wqg_ref), (wo_hbm, wo_ref), (x_hbm, x_v), (dy_hbm, dy_v)])
    ]
    for copy in small_in + large_in:
        copy.start()

    @pl.when(jnp.logical_not(has_prev))
    def _():
        lo_v[...] = jnp.zeros_like(lo_v)
        gprev_v[...] = jnp.zeros_like(gprev_v)
        band_v[:, :TOK] = jnp.zeros((TOK, TOK, CH), BF16)

    @pl.when(jnp.logical_not(has_next))
    def _():
        hi_v[...] = jnp.zeros_like(hi_v)
        gnext_v[...] = jnp.zeros_like(gnext_v)
        band_v[:, 2 * TOK :] = jnp.zeros((TOK, TOK, CH), BF16)

    for copy in small_in:
        copy.wait()

    g_prev = jnp.maximum(me - 1, 0)
    g_next = jnp.minimum(me + 1, blocks - 1)
    run_prev, run_own, run_next = totals_of(counts, g_prev), totals_of(counts, me), totals_of(counts, g_next)
    atom = iota((EXT, 32), 0)
    is_lo, is_hi = atom < HALO, atom >= HALO + BLOCK
    local = jnp.where(is_lo, atom + (BLOCK - HALO), jnp.where(is_hi, atom - (HALO + BLOCK), atom - HALO))
    token = jnp.where(is_lo, 0, jnp.where(is_hi, 2 * TOK, TOK))
    for j in range(TOK):
        limit = jnp.where(is_lo, run_prev[j], jnp.where(is_hi, run_next[j], run_own[j]))
        token = token + (limit <= local).astype(jnp.int32)
    key_hot32 = (token == iota((EXT, 32), 1)).astype(F32)
    key_hot = key_hot32.astype(BF16)

    lane = iota((TOK, LANES), 1)
    query = (lane // KEYS) * WIN + lane % WIN
    query_token = jnp.zeros((TOK, LANES), jnp.int32)
    for j in range(TOK):
        query_token = query_token + (run_own[j] <= query).astype(jnp.int32)

    slot_row = iota((32, LANES), 0)
    mask_rows = jnp.zeros((32, LANES), F32)
    for u in range(3 * TOK):
        where_to = me * TOK + u - TOK
        bit = mask[jnp.clip(where_to, 0, blocks * TOK - 1)]
        bit = jnp.where(jnp.logical_and(where_to >= 0, where_to < blocks * TOK), bit, 0)
        mask_rows = jnp.where(slot_row == u, bit.astype(F32), mask_rows)
    valid = nn(key_hot, mask_rows.astype(BF16))

    pl.semaphore_wait(
        barrier, (cols - 1) + (rows - 1) + far_next.astype(jnp.int32) + far_prev.astype(jnp.int32)
    )

    def to_next(i):
        return pltpu.make_async_remote_copy(
            src_ref=x_hbm.at[pl.ds(i * STEP, STEP), pl.ds(BLOCK - HALO, HALO)],
            dst_ref=lo_v.at[pl.ds(i * STEP, STEP)],
            send_sem=lo_send.at[i], recv_sem=lo_recv.at[i],
            device_id=next_id, device_id_type=MESH)

    def to_prev(i):
        return pltpu.make_async_remote_copy(
            src_ref=x_hbm.at[pl.ds(i * STEP, STEP), pl.ds(0, HALO)],
            dst_ref=hi_v.at[pl.ds(i * STEP, STEP)],
            send_sem=hi_send.at[i], recv_sem=hi_recv.at[i],
            device_id=prev_id, device_id_type=MESH)

    def grad_to_prev(i):
        return pltpu.make_async_remote_copy(
            src_ref=glo_v.at[pl.ds(i * STEP, STEP)],
            dst_ref=gnext_v.at[pl.ds(i * STEP, STEP)],
            send_sem=glo_send.at[i], recv_sem=gn_recv.at[i],
            device_id=prev_id, device_id_type=MESH)

    def grad_to_next(i):
        return pltpu.make_async_remote_copy(
            src_ref=ghi_v.at[pl.ds(i * STEP, STEP)],
            dst_ref=gprev_v.at[pl.ds(i * STEP, STEP)],
            send_sem=ghi_send.at[i], recv_sem=gp_recv.at[i],
            device_id=next_id, device_id_type=MESH)

    delta = rows * col - cols * row

    def inside(j):
        return jnp.logical_and(j >= 0, j < cols)

    def clamped(j):
        return jnp.clip(j, 0, cols - 1)

    def band_refs(d, j, wide, first):
        k = d - 1 + first
        return (
            pair_hbm.at[pl.ds(j * TOK, TOK), pl.ds(pl.multiple_of(k * TOK, TOK), wide * TOK)],
            band_v.at[:, pl.ds(first * TOK, wide * TOK)])

    def band_copy(d, j, wide, first):
        src, dst = band_refs(d, j, wide, first)
        return pltpu.make_async_remote_copy(
            src_ref=src, dst_ref=dst,
            send_sem=band_send.at[d + 1], recv_sem=band_recv.at[0 if wide > 1 else 1],
            device_id=(row, j), device_id_type=MESH)

    def band_local(d, j, wide, first):
        src, dst = band_refs(d, j, wide, first)
        return pltpu.make_async_copy(src, dst, band_send.at[d + 1])

    def send_band(d, wide, first):
        j = delta + d

        @pl.when(jnp.logical_and(inside(j), j != col))
        def _():
            band_copy(d, clamped(j), wide, first).start()

        @pl.when(jnp.logical_and(inside(j), j == col))
        def _():
            band_local(d, clamped(j), wide, first).start()

    def band_sent(d, wide, first):
        j = delta + d

        @pl.when(jnp.logical_and(inside(j), j != col))
        def _():
            band_copy(d, clamped(j), wide, first).wait_send()

    def all_readers(act):
        @pl.loop(1, rows - 1)
        def _(d):
            act(d, 3, 0)

        act(0, 2, 1)
        act(rows - 1, 2, 0)
        act(-1, 1, 2)
        act(rows, 1, 0)

    owner = me // rows
    mine = me % rows
    side_low = jnp.logical_and(mine == 0, has_prev)
    side_high = jnp.logical_and(mine == rows - 1, has_next)

    def receive_band(cond, source, d, wide, first):
        @pl.when(jnp.logical_and(cond, source != col))
        def _():
            band_copy(d, col, wide, first).wait_recv()

        @pl.when(jnp.logical_and(cond, source == col))
        def _():
            band_local(d, col, wide, first).wait()

    def piece_copy(target, d, wide, first):
        at = pl.ds(first * TOK, wide * TOK)
        return pltpu.make_async_remote_copy(
            src_ref=bandgrad_v.at[:, at], dst_ref=piece_v.at[d + 1, :, at],
            send_sem=piece_send.at[0 if wide > 1 else 1], recv_sem=piece_recv.at[d + 1],
            device_id=(row, target), device_id_type=MESH)

    def to_owners(act):
        act(jnp.logical_and(mine > 0, mine < rows - 1), owner, mine, 3, 0)
        act(mine == 0, owner, 0, 2, 1)
        act(mine == rows - 1, owner, rows - 1, 2, 0)
        act(side_high, owner + 1, -1, 1, 2)
        act(side_low, owner - 1, rows, 1, 0)

    def send_rows(i):
        @pl.when(has_next)
        def _():
            to_next(i).start()

        @pl.when(has_prev)
        def _():
            to_prev(i).start()

    send_rows(0)
    all_readers(send_band)

    @pl.loop(1, AHEAD)
    def _(i):
        send_rows(i)

    to_owners(receive_band)

    def band_normed():
        return normalize(
            jnp.concatenate(
                [band_v[t, s * TOK : (s + 1) * TOK].astype(F32) for s in range(3) for t in range(TOK)], axis=0))

    pw_v[...] = jnp.concatenate([pwt_v[...], jnp.zeros((8 - HEADS, CH), F32)], axis=0).T
    head_lane = (iota((CH, LANES), 1) % KEYS) // WIN
    spread_weight = jnp.zeros((CH, LANES), F32)
    for h in range(HEADS):
        spread_weight = jnp.where(head_lane == h, pw_v[:, h : h + 1], spread_weight)
    normed, _ = band_normed()
    projected = nn(normed, spread_weight, HI)
    table = []
    for s in range(3):
        part = jnp.zeros((TOK, LANES), F32)
        for t in range(TOK):
            at = (s * TOK + t) * TOK
            part = jnp.where(query_token == t, projected[at : at + TOK], part)
        table.append(part)
    table = jnp.concatenate(table, axis=0)
    table = jnp.concatenate([table, jnp.zeros((8, LANES), F32)], axis=0).astype(BF16)
    bias = jnp.where(valid > 0.5, nn(key_hot, table), nn(key_hot, table) + MASKED)
    for w in range(2):
        bt_v[w] = bias[w * WIN : w * WIN + KEYS, w * KEYS : (w + 1) * KEYS]
    dbt_v[...] = jnp.zeros_like(dbt_v)
    pair_out[...] = jnp.zeros_like(pair_out)

    head_of = iota((WIN, CH), 1) // WIN
    head_mask = [(head_of == h).astype(BF16) for h in range(HEADS)]

    def expand(a):
        return jnp.concatenate(
            [a[w * WIN : (w + 1) * WIN] * head_mask[h] for w in range(2) for h in range(HEADS)], axis=0)

    def fold(a):
        out = a[:WIN]
        for h in range(1, HEADS):
            out = jnp.where(head_of == h, a[h * WIN : (h + 1) * WIN], out)
        return out

    gap = jnp.zeros((WIN, KEYS), BF16)

    def both(a0, a1):
        return jnp.concatenate(
            [jnp.concatenate([a0, gap], axis=0), jnp.concatenate([gap, a1], axis=0)], axis=1)

    for copy in large_in:
        copy.wait()

    def finish(i):
        @pl.when(has_next)
        def _():
            grad_to_prev(i).wait_recv()

        @pl.when(has_prev)
        def _():
            grad_to_next(i).wait_recv()

        part = pl.ds(i * STEP, STEP)
        from_prev = gprev_v[part].astype(F32)
        from_next = gnext_v[part].astype(F32)
        cut = BLOCK - HALO
        grad_v[part, 0:cut] = (center_v[part, 0:cut] + from_prev[:, :cut]).astype(BF16)
        grad_v[part, cut:HALO] = (
            center_v[part, cut:HALO] + from_prev[:, cut:] + from_next[:, : HALO - cut]).astype(BF16)
        grad_v[part, HALO:BLOCK] = (center_v[part, HALO:BLOCK] + from_next[:, HALO - cut :]).astype(BF16)

    def first_pass(i):
        @pl.when(i + AHEAD < chunks)
        def _():
            send_rows(i + AHEAD)

        part = pl.ds(i * STEP, STEP)
        x3 = x_v[part]
        x = x3.reshape(STEP * BLOCK, CH)
        dy = dy_v[part].reshape(STEP * BLOCK, CH)
        query_gate = nn(x, wqg_ref[...])
        q_v[part] = query_gate[:, :CH].astype(BF16).reshape(STEP, BLOCK, CH)
        gate_v[...] = jax.nn.sigmoid(query_gate[:, CH:]).reshape(STEP, BLOCK, CH)
        dgated_v[...] = nt(dy, wo_ref[...]).astype(BF16).reshape(STEP, BLOCK, CH)
        kv_v[part, HALO : HALO + BLOCK] = nn(x, wkv_ref[...]).astype(BF16).reshape(STEP, BLOCK, 2 * CH)

        @pl.when(has_prev)
        def _():
            to_next(i).wait_recv()

        @pl.when(has_next)
        def _():
            to_prev(i).wait_recv()

        lo = lo_v[part].reshape(STEP * HALO, CH)
        hi = hi_v[part].reshape(STEP * HALO, CH)
        kv_v[part, :HALO] = nn(lo, wkv_ref[...]).astype(BF16).reshape(STEP, HALO, 2 * CH)
        kv_v[part, HALO + BLOCK :] = nn(hi, wkv_ref[...]).astype(BF16).reshape(STEP, HALO, 2 * CH)

        for s in range(STEP):
            at = i * STEP + s
            datt = (dgated_v[s].astype(F32) * gate_v[s]).astype(BF16)
            datt_v[at] = datt
            logit_v[s] = nt(kv_v[at, :, :CH], expand(q_v[at]))
            dprob_v[s] = nt(kv_v[at, :, CH:], expand(datt))
        for w in range(2):
            ks = slice(w * WIN, w * WIN + KEYS)
            ls = slice(w * KEYS, (w + 1) * KEYS)
            for s in range(STEP):
                at = i * STEP + s
                score = logit_v[s, ks, ls] * SCALE + bt_v[w]
                e = jnp.exp(score - jnp.max(score, axis=0, keepdims=True))
                p = e * (1.0 / jnp.sum(e, axis=0, keepdims=True))
                t = dprob_v[s, ks, ls] * p
                ds = t - p * jnp.sum(t, axis=0, keepdims=True)
                dbt_v[w] += ds
                prob_v[at, w] = p.astype(BF16)
                dscore_v[at, w] = ds.astype(BF16)
        for s in range(STEP):
            at = i * STEP + s
            gate = gate_v[s]
            mixed = [fold(tn(prob_v[at, w], kv_v[at, w * WIN : w * WIN + KEYS, CH:])) for w in range(2)]
            attended = jnp.concatenate(mixed, axis=0)
            gated_v[s] = (attended * gate).astype(BF16)
            dgate_v[at] = (dgated_v[s].astype(F32) * attended * (gate * (1.0 - gate))).astype(BF16)

        out = x.astype(F32) + nn(gated_v[...].reshape(STEP * BLOCK, CH), wo_ref[...])
        upd_v[part] = out.astype(BF16).reshape(STEP, BLOCK, CH)

    def second_pass(i):
        part = pl.ds(i * STEP, STEP)
        for s in range(STEP):
            at = i * STEP + s
            dkv_v[s, :, :CH] = (nn(both(dscore_v[at, 0], dscore_v[at, 1]), expand(q_v[at])) * SCALE).astype(BF16)
            dkv_v[s, :, CH:] = nn(both(prob_v[at, 0], prob_v[at, 1]), expand(datt_v[at])).astype(BF16)

        glo = nt(dkv_v[:, :HALO].reshape(STEP * HALO, 2 * CH), wkv_ref[...])
        glo_v[part] = glo.astype(BF16).reshape(STEP, HALO, CH)
        ghi = nt(dkv_v[:, HALO + BLOCK :].reshape(STEP * HALO, 2 * CH), wkv_ref[...])
        ghi_v[part] = ghi.astype(BF16).reshape(STEP, HALO, CH)

        @pl.when(has_prev)
        def _():
            grad_to_prev(i).start()

        @pl.when(has_next)
        def _():
            grad_to_next(i).start()

        for s in range(STEP):
            at = i * STEP + s
            for w in range(2):
                dq = fold(tn(dscore_v[at, w], kv_v[at, w * WIN : w * WIN + KEYS, :CH]))
                dq_v[s, w * WIN : (w + 1) * WIN] = (dq * SCALE).astype(BF16)
        dquery = dq_v[...].reshape(STEP * BLOCK, CH)
        dgate = dgate_v[part].reshape(STEP * BLOCK, CH)
        own = nt(dkv_v[:, HALO : HALO + BLOCK].reshape(STEP * BLOCK, 2 * CH), wkv_ref[...])
        own = own + nt(jnp.concatenate([dquery, dgate], axis=1), wqg_ref[...])
        own = own + dy_v[part].reshape(STEP * BLOCK, CH).astype(F32)
        center_v[part] = own.reshape(STEP, BLOCK, CH)

        @pl.when(i >= LAG)
        def _():
            finish(i - LAG)

    def a_copy(peer, slot):
        return pltpu.make_async_remote_copy(
            src_ref=part_a, dst_ref=red_a.at[slot],
            send_sem=a_send.at[peer], recv_sem=a_recv.at[slot],
            device_id=(row, peer), device_id_type=MESH)

    def b_copy(peer, slot):
        return pltpu.make_async_remote_copy(
            src_ref=part_b, dst_ref=red_b.at[slot],
            send_sem=b_send.at[peer], recv_sem=b_recv.at[slot],
            device_id=(peer, col), device_id_type=MESH)

    @pl.loop(0, chunks)
    def _(i):
        first_pass(i)

        @pl.when(i >= DELAY)
        def _():
            second_pass(i - DELAY)

    gap32 = jnp.zeros((WIN, KEYS), F32)
    dbias = jnp.concatenate(
        [jnp.concatenate([dbt_v[0], gap32], axis=0), jnp.concatenate([gap32, dbt_v[1]], axis=0)], axis=1)
    dtable = tn(key_hot32, dbias, HI)[: 3 * TOK]
    by_token = jnp.concatenate(
        [
            jnp.where(query_token == t, dtable[s * TOK : (s + 1) * TOK], 0.0)
            for s in range(3) for t in range(TOK)
        ], axis=0)
    head_row = (iota((8, LANES), 1) % KEYS) // WIN
    to_head = (head_row == iota((8, LANES), 0)).astype(F32)
    dbias_rows = nt(to_head, by_token, HI).astype(BF16).astype(F32)
    normed, rstd = band_normed()
    part_a[...] = nn(dbias_rows, normed, HI)
    red_a[col] = part_a[...]

    @pl.loop(1, cols)
    def _(d):
        a_copy(lax.rem(col + d, cols), col).start()

    weight = jnp.concatenate([pwt_v[...], jnp.zeros((8 - HEADS, CH), F32)], axis=0)
    dnormed = tn(dbias_rows, weight, HI)
    dvalues = rstd * (
        dnormed - jnp.mean(dnormed, axis=1, keepdims=True)
        - normed * jnp.mean(dnormed * normed, axis=1, keepdims=True))
    for s in range(3):
        for t in range(TOK):
            at = (s * TOK + t) * TOK
            bandgrad_v[t, s * TOK : (s + 1) * TOK] = dvalues[at : at + TOK].astype(BF16)

    def send_piece(cond, target, d, wide, first):
        @pl.when(jnp.logical_and(cond, target != col))
        def _():
            piece_copy(target, d, wide, first).start()

        @pl.when(jnp.logical_and(cond, target == col))
        def _():
            piece_v[d + 1] = bandgrad_v[...]

    to_owners(send_piece)

    @pl.loop(chunks - DELAY, chunks - DELAY + HALF)
    def _(i):
        second_pass(i)

    @pl.loop(1, cols)
    def _(d):
        source = lax.rem(col + d, cols)
        a_copy(source, source).wait_recv()

    total = red_a[0]
    for j in range(1, cols):
        total = total + red_a[j]
    part_b[...] = total
    red_b[row] = total

    @pl.loop(1, rows)
    def _(d):
        b_copy(lax.rem(row + d, rows), row).start()

    @pl.loop(chunks - DELAY + HALF, chunks)
    def _(i):
        second_pass(i)

    def place(d, wide, first):
        j = delta + d

        @pl.when(jnp.logical_and(inside(j), j != col))
        def _():
            piece_copy(clamped(j), d, wide, first).wait_recv()

        @pl.when(inside(j))
        def _():
            for s in range(first, first + wide):
                at = pl.ds(pl.multiple_of((d + s - 1) * TOK, TOK), TOK)
                for t in range(TOK):
                    pair_out[clamped(j) * TOK + t, at] = piece_v[d + 1, t, s * TOK : (s + 1) * TOK]

    all_readers(place)

    @pl.loop(chunks - LAG, chunks)
    def _(i):
        finish(i)

    def sent_piece(cond, target, d, wide, first):
        @pl.when(jnp.logical_and(cond, target != col))
        def _():
            piece_copy(target, d, wide, first).wait_send()

    to_owners(sent_piece)
    all_readers(band_sent)

    @pl.loop(0, chunks)
    def _(i):
        @pl.when(has_next)
        def _():
            to_next(i).wait_send()
            grad_to_next(i).wait_send()

        @pl.when(has_prev)
        def _():
            to_prev(i).wait_send()
            grad_to_prev(i).wait_send()

    @pl.loop(1, cols)
    def _(d):
        a_copy(lax.rem(col + d, cols), col).wait_send()

    @pl.loop(1, rows)
    def _(d):
        source = lax.rem(row + d, rows)
        b_copy(source, source).wait_recv()

    total = red_b[0]
    for j in range(1, rows):
        total = total + red_b[j]
    wgrad_out[...] = total

    @pl.loop(1, rows)
    def _(d):
        b_copy(lax.rem(row + d, rows), row).wait_send()


def final_kernel(upd_in, grad_in, pair_in, wsum, upd_out, grad_out, pair_out, wgrad, sems):
    copies = [
        pltpu.make_async_copy(src, dst, sems.at[n])
        for n, (src, dst) in enumerate([(pair_in, pair_out), (upd_in, upd_out), (grad_in, grad_out)])
    ]
    for copy in copies:
        copy.start()
    wgrad[...] = wsum[:HEADS]
    for copy in copies:
        copy.wait()


def on_device(rows, cols, atom_rows, pair_rep, wqg, wkv, wo, pw, counts, token_mask, cotangent):
    samples = atom_rows.shape[0]
    chunks = samples // STEP
    vmem = pl.BlockSpec(memory_space=pltpu.VMEM)
    hbm = pl.BlockSpec(memory_space=pltpu.HBM)
    own = (samples, BLOCK, CH)
    halo = (samples, HALO, CH)
    dma = pltpu.SemaphoreType.DMA
    upd, grad, pair, wsum = pl.pallas_call(
        functools.partial(main_kernel, rows, cols, samples),
        out_shape=(
            jax.ShapeDtypeStruct(own, BF16),
            jax.ShapeDtypeStruct(own, BF16),
            jax.ShapeDtypeStruct(pair_rep.shape, BF16),
            jax.ShapeDtypeStruct((8, CH), F32),
        ),
        in_specs=[hbm] * 9,
        out_specs=(vmem,) * 4,
        scratch_shapes=[
            pltpu.SMEM((TOK, rows * cols), jnp.int32), pltpu.SMEM((rows * cols * TOK,), jnp.int32),
            pltpu.VMEM((CH, 2 * CH), BF16), pltpu.VMEM((CH, 2 * CH), BF16), pltpu.VMEM((CH, CH), BF16),
            pltpu.VMEM((HEADS, CH), F32), pltpu.VMEM((CH, 8), F32),
            pltpu.VMEM(own, BF16), pltpu.VMEM(own, BF16),
            pltpu.VMEM(halo, BF16), pltpu.VMEM(halo, BF16),
            pltpu.VMEM(halo, BF16), pltpu.VMEM(halo, BF16),
            pltpu.VMEM(halo, BF16), pltpu.VMEM(halo, BF16),
            pltpu.VMEM(own, F32),
            pltpu.VMEM((TOK, 3 * TOK, CH), BF16), pltpu.VMEM((TOK, 3 * TOK, CH), BF16),
            pltpu.VMEM((rows + 2, TOK, 3 * TOK, CH), BF16),
            pltpu.VMEM((2, KEYS, KEYS), F32), pltpu.VMEM((2, KEYS, KEYS), F32),
            pltpu.VMEM((samples, EXT, 2 * CH), BF16), pltpu.VMEM((STEP, EXT, 2 * CH), BF16),
            pltpu.VMEM(own, BF16), pltpu.VMEM((STEP, BLOCK, CH), F32),
            pltpu.VMEM((STEP, BLOCK, CH), BF16), pltpu.VMEM((STEP, BLOCK, CH), BF16),
            pltpu.VMEM(own, BF16), pltpu.VMEM((STEP, BLOCK, CH), BF16), pltpu.VMEM(own, BF16),
            pltpu.VMEM((samples, 2, KEYS, KEYS), BF16), pltpu.VMEM((samples, 2, KEYS, KEYS), BF16),
            pltpu.VMEM((STEP, EXT, LANES), F32), pltpu.VMEM((STEP, EXT, LANES), F32),
            pltpu.VMEM((cols, 8, CH), F32), pltpu.VMEM((rows, 8, CH), F32),
            pltpu.VMEM((8, CH), F32), pltpu.VMEM((8, CH), F32),
            dma((8,)),
            dma((chunks,)), dma((chunks,)), dma((chunks,)), dma((chunks,)),
            dma((chunks,)), dma((chunks,)), dma((chunks,)), dma((chunks,)),
            dma((rows + 2,)), dma((2,)), dma((2,)), dma((rows + 2,)),
            dma((cols,)), dma((cols,)), dma((rows,)), dma((rows,)),
        ],
        compiler_params=pltpu.CompilerParams(
            collective_id=0, has_side_effects=True, vmem_limit_bytes=40 * 2**20),
    )(*[
        pltpu.with_memory_space_constraint(array, pltpu.HBM)
        for array in (counts.T, token_mask, atom_rows, pair_rep, wqg, wkv, wo, pw.T, cotangent)
    ])
    upd, grad, pair_grad, wgrad = pl.pallas_call(
        final_kernel,
        out_shape=(
            jax.ShapeDtypeStruct(own, BF16),
            jax.ShapeDtypeStruct(own, BF16),
            jax.ShapeDtypeStruct(pair_rep.shape, BF16),
            jax.ShapeDtypeStruct((HEADS, CH), F32),
        ),
        in_specs=[vmem, vmem, vmem, vmem],
        out_specs=(hbm, hbm, hbm, vmem),
        scratch_shapes=[dma((3,))],
        compiler_params=pltpu.CompilerParams(vmem_limit_bytes=8 * 2**20),
    )(upd, grad, pair, wsum)
    return upd, grad, pair_grad, wgrad.T


def solution(mesh):
    rows, cols = mesh.shape["row"], mesh.shape["col"]
    atoms = P(None, ("row", "col"), None)
    pairs = P("row", "col", None)
    return jax.shard_map(
        functools.partial(on_device, rows, cols),
        mesh=mesh,
        in_specs=(atoms, pairs, P(), P(), P(), P(), P(), P(), atoms),
        out_specs=(atoms, atoms, pairs, P()),
        check_vma=False,
    )
```

```python
import functools
import math

import jax
import jax.numpy as jnp
from jax import lax
from jax.experimental import pallas as pl
from jax.experimental.pallas import tpu as pltpu
from jax.sharding import PartitionSpec as P

BLOCK = 64
TOK = 8
HEADS = 4
WIN = 32
KEYS = 128
HALO = 48
CH = 128
EXT = BLOCK + 2 * HALO
LANES = 2 * HEADS * WIN
EPS = 1e-05
MASKED = -1000000000.0
SCALE = 1.0 / math.sqrt(CH // HEADS)
STEP = 12
AHEAD = 2
LAG = 3
DELAY = 1
HALF = 1

F32 = jnp.float32
BF16 = jnp.bfloat16
HI = lax.Precision.HIGHEST
MESH = pl.DeviceIdType.MESH


def nn(a, b, precision=None):
    return lax.dot_general(a, b, (((1,), (0,)), ((), ())), precision=precision, preferred_element_type=F32)


def nt(a, b, precision=None):
    return lax.dot_general(a, b, (((1,), (1,)), ((), ())), precision=precision, preferred_element_type=F32)


def tn(a, b, precision=None):
    return lax.dot_general(a, b, (((0,), (0,)), ((), ())), precision=precision, preferred_element_type=F32)


def iota(shape, dim):
    return lax.broadcasted_iota(jnp.int32, shape, dim)


def normalize(values):
    centered = values - jnp.mean(values, axis=1, keepdims=True)
    rstd = lax.rsqrt(jnp.mean(centered * centered, axis=1, keepdims=True) + EPS)
    return centered * rstd, rstd


def totals_of(counts, group):
    running, total = [], 0
    for j in range(TOK):
        total = total + counts[j, group]
        running.append(total)
    return running


def main_kernel(
    rows, cols, samples,
    counts_hbm, mask_hbm, x_hbm, pair_hbm, wqg_hbm, wkv_hbm, wo_hbm, pw_hbm, dy_hbm,
    upd_v, grad_v, pair_out, wgrad_out,
    counts, mask, wqg_ref, wkv_ref, wo_ref, pwt_v, pw_v,
    x_v, dy_v, lo_v, hi_v, glo_v, ghi_v, gprev_v, gnext_v, center_v,
    band_v, bandgrad_v, piece_v, bt_v, dbt_v, kv_v, dkv_v, q_v, gate_v, dgated_v, gated_v, dgate_v, dq_v,
    datt_v, prob_v, dscore_v, logit_v, dprob_v,
    red_a, red_b, part_a, part_b,
    in_sem, lo_send, hi_send, lo_recv, hi_recv, glo_send, ghi_send, gp_recv, gn_recv,
    band_send, band_recv, piece_send, piece_recv, a_send, a_recv, b_send, b_recv,
):
    chunks = samples // STEP
    blocks = rows * cols
    row = lax.axis_index("row")
    col = lax.axis_index("col")
    me = row * cols + col
    has_prev = me > 0
    has_next = me < blocks - 1
    before = jnp.maximum(me - 1, 0)
    after = jnp.minimum(me + 1, blocks - 1)
    prev_id = (before // cols, before % cols)
    next_id = (after // cols, after % cols)

    barrier = pltpu.get_barrier_semaphore()

    @pl.loop(1, cols)
    def _(d):
        pl.semaphore_signal(barrier, inc=1, device_id=(row, lax.rem(col + d, cols)), device_id_type=MESH)

    @pl.loop(1, rows)
    def _(d):
        pl.semaphore_signal(barrier, inc=1, device_id=(lax.rem(row + d, rows), col), device_id_type=MESH)

    far_next = jnp.logical_and(col == cols - 1, has_next)
    far_prev = jnp.logical_and(col == 0, has_prev)

    @pl.when(far_next)
    def _():
        pl.semaphore_signal(barrier, inc=1, device_id=next_id, device_id_type=MESH)

    @pl.when(far_prev)
    def _():
        pl.semaphore_signal(barrier, inc=1, device_id=prev_id, device_id_type=MESH)

    small_in = [
        pltpu.make_async_copy(src, dst, in_sem.at[n])
        for n, (src, dst) in enumerate([(counts_hbm, counts), (mask_hbm, mask), (pw_hbm, pwt_v)])
    ]
    large_in = [
        pltpu.make_async_copy(src, dst, in_sem.at[3 + n])
        for n, (src, dst) in enumerate(
            [(wkv_hbm, wkv_ref), (wqg_hbm, wqg_ref), (wo_hbm, wo_ref), (x_hbm, x_v), (dy_hbm, dy_v)])
    ]
    for copy in small_in + large_in:
        copy.start()

    @pl.when(jnp.logical_not(has_prev))
    def _():
        lo_v[...] = jnp.zeros_like(lo_v)
        gprev_v[...] = jnp.zeros_like(gprev_v)
        band_v[:, :TOK] = jnp.zeros((TOK, TOK, CH), BF16)

    @pl.when(jnp.logical_not(has_next))
    def _():
        hi_v[...] = jnp.zeros_like(hi_v)
        gnext_v[...] = jnp.zeros_like(gnext_v)
        band_v[:, 2 * TOK :] = jnp.zeros((TOK, TOK, CH), BF16)

    for copy in small_in:
        copy.wait()

    g_prev = jnp.maximum(me - 1, 0)
    g_next = jnp.minimum(me + 1, blocks - 1)
    run_prev, run_own, run_next = totals_of(counts, g_prev), totals_of(counts, me), totals_of(counts, g_next)
    atom = iota((EXT, 32), 0)
    is_lo, is_hi = atom < HALO, atom >= HALO + BLOCK
    local = jnp.where(is_lo, atom + (BLOCK - HALO), jnp.where(is_hi, atom - (HALO + BLOCK), atom - HALO))
    token = jnp.where(is_lo, 0, jnp.where(is_hi, 2 * TOK, TOK))
    for j in range(TOK):
        limit = jnp.where(is_lo, run_prev[j], jnp.where(is_hi, run_next[j], run_own[j]))
        token = token + (limit <= local).astype(jnp.int32)
    key_hot32 = (token == iota((EXT, 32), 1)).astype(F32)
    key_hot = key_hot32.astype(BF16)

    lane = iota((TOK, LANES), 1)
    query = (lane // KEYS) * WIN + lane % WIN
    query_token = jnp.zeros((TOK, LANES), jnp.int32)
    for j in range(TOK):
        query_token = query_token + (run_own[j] <= query).astype(jnp.int32)

    slot_row = iota((32, LANES), 0)
    mask_rows = jnp.zeros((32, LANES), F32)
    for u in range(3 * TOK):
        where_to = me * TOK + u - TOK
        bit = mask[jnp.clip(where_to, 0, blocks * TOK - 1)]
        bit = jnp.where(jnp.logical_and(where_to >= 0, where_to < blocks * TOK), bit, 0)
        mask_rows = jnp.where(slot_row == u, bit.astype(F32), mask_rows)
    valid = nn(key_hot, mask_rows.astype(BF16))

    pl.semaphore_wait(
        barrier, (cols - 1) + (rows - 1) + far_next.astype(jnp.int32) + far_prev.astype(jnp.int32)
    )

    def to_next(i):
        return pltpu.make_async_remote_copy(
            src_ref=x_hbm.at[pl.ds(i * STEP, STEP), pl.ds(BLOCK - HALO, HALO)],
            dst_ref=lo_v.at[pl.ds(i * STEP, STEP)],
            send_sem=lo_send.at[i], recv_sem=lo_recv.at[i],
            device_id=next_id, device_id_type=MESH)

    def to_prev(i):
        return pltpu.make_async_remote_copy(
            src_ref=x_hbm.at[pl.ds(i * STEP, STEP), pl.ds(0, HALO)],
            dst_ref=hi_v.at[pl.ds(i * STEP, STEP)],
            send_sem=hi_send.at[i], recv_sem=hi_recv.at[i],
            device_id=prev_id, device_id_type=MESH)

    def grad_to_prev(i):
        return pltpu.make_async_remote_copy(
            src_ref=glo_v.at[pl.ds(i * STEP, STEP)],
            dst_ref=gnext_v.at[pl.ds(i * STEP, STEP)],
            send_sem=glo_send.at[i], recv_sem=gn_recv.at[i],
            device_id=prev_id, device_id_type=MESH)

    def grad_to_next(i):
        return pltpu.make_async_remote_copy(
            src_ref=ghi_v.at[pl.ds(i * STEP, STEP)],
            dst_ref=gprev_v.at[pl.ds(i * STEP, STEP)],
            send_sem=ghi_send.at[i], recv_sem=gp_recv.at[i],
            device_id=next_id, device_id_type=MESH)

    delta = rows * col - cols * row

    def inside(j):
        return jnp.logical_and(j >= 0, j < cols)

    def clamped(j):
        return jnp.clip(j, 0, cols - 1)

    def band_refs(d, j, wide, first):
        k = d - 1 + first
        return (
            pair_hbm.at[pl.ds(j * TOK, TOK), pl.ds(pl.multiple_of(k * TOK, TOK), wide * TOK)],
            band_v.at[:, pl.ds(first * TOK, wide * TOK)])

    def band_copy(d, j, wide, first):
        src, dst = band_refs(d, j, wide, first)
        return pltpu.make_async_remote_copy(
            src_ref=src, dst_ref=dst,
            send_sem=band_send.at[d + 1], recv_sem=band_recv.at[0 if wide > 1 else 1],
            device_id=(row, j), device_id_type=MESH)

    def band_local(d, j, wide, first):
        src, dst = band_refs(d, j, wide, first)
        return pltpu.make_async_copy(src, dst, band_send.at[d + 1])

    def send_band(d, wide, first):
        j = delta + d

        @pl.when(jnp.logical_and(inside(j), j != col))
        def _():
            band_copy(d, clamped(j), wide, first).start()

        @pl.when(jnp.logical_and(inside(j), j == col))
        def _():
            band_local(d, clamped(j), wide, first).start()

    def band_sent(d, wide, first):
        j = delta + d

        @pl.when(jnp.logical_and(inside(j), j != col))
        def _():
            band_copy(d, clamped(j), wide, first).wait_send()

    def all_readers(act):
        @pl.loop(1, rows - 1)
        def _(d):
            act(d, 3, 0)

        act(0, 2, 1)
        act(rows - 1, 2, 0)
        act(-1, 1, 2)
        act(rows, 1, 0)

    owner = me // rows
    mine = me % rows
    side_low = jnp.logical_and(mine == 0, has_prev)
    side_high = jnp.logical_and(mine == rows - 1, has_next)

    def receive_band(cond, source, d, wide, first):
        @pl.when(jnp.logical_and(cond, source != col))
        def _():
            band_copy(d, col, wide, first).wait_recv()

        @pl.when(jnp.logical_and(cond, source == col))
        def _():
            band_local(d, col, wide, first).wait()

    def piece_copy(target, d, wide, first):
        at = pl.ds(first * TOK, wide * TOK)
        return pltpu.make_async_remote_copy(
            src_ref=bandgrad_v.at[:, at], dst_ref=piece_v.at[d + 1, :, at],
            send_sem=piece_send.at[0 if wide > 1 else 1], recv_sem=piece_recv.at[d + 1],
            device_id=(row, target), device_id_type=MESH)

    def to_owners(act):
        act(jnp.logical_and(mine > 0, mine < rows - 1), owner, mine, 3, 0)
        act(mine == 0, owner, 0, 2, 1)
        act(mine == rows - 1, owner, rows - 1, 2, 0)
        act(side_high, owner + 1, -1, 1, 2)
        act(side_low, owner - 1, rows, 1, 0)

    def send_rows(i):
        @pl.when(has_next)
        def _():
            to_next(i).start()

        @pl.when(has_prev)
        def _():
            to_prev(i).start()

    send_rows(0)
    all_readers(send_band)

    @pl.loop(1, AHEAD)
    def _(i):
        send_rows(i)

    to_owners(receive_band)

    def band_normed():
        return normalize(
            jnp.concatenate(
                [band_v[t, s * TOK : (s + 1) * TOK].astype(F32) for s in range(3) for t in range(TOK)], axis=0))

    pw_v[...] = jnp.concatenate([pwt_v[...], jnp.zeros((8 - HEADS, CH), F32)], axis=0).T
    head_lane = (iota((CH, LANES), 1) % KEYS) // WIN
    spread_weight = jnp.zeros((CH, LANES), F32)
    for h in range(HEADS):
        spread_weight = jnp.where(head_lane == h, pw_v[:, h : h + 1], spread_weight)
    normed, _ = band_normed()
    projected = nn(normed, spread_weight, HI)
    table = []
    for s in range(3):
        part = jnp.zeros((TOK, LANES), F32)
        for t in range(TOK):
            at = (s * TOK + t) * TOK
            part = jnp.where(query_token == t, projected[at : at + TOK], part)
        table.append(part)
    table = jnp.concatenate(table, axis=0)
    table = jnp.concatenate([table, jnp.zeros((8, LANES), F32)], axis=0).astype(BF16)
    bias = jnp.where(valid > 0.5, nn(key_hot, table), nn(key_hot, table) + MASKED)
    for w in range(2):
        bt_v[w] = bias[w * WIN : w * WIN + KEYS, w * KEYS : (w + 1) * KEYS]
    dbt_v[...] = jnp.zeros_like(dbt_v)
    pair_out[...] = jnp.zeros_like(pair_out)

    head_of = iota((WIN, CH), 1) // WIN
    head_mask = [(head_of == h).astype(BF16) for h in range(HEADS)]

    def expand(a):
        return jnp.concatenate(
            [a[w * WIN : (w + 1) * WIN] * head_mask[h] for w in range(2) for h in range(HEADS)], axis=0)

    def fold(a):
        out = a[:WIN]
        for h in range(1, HEADS):
            out = jnp.where(head_of == h, a[h * WIN : (h + 1) * WIN], out)
        return out

    gap = jnp.zeros((WIN, KEYS), BF16)

    def both(a0, a1):
        return jnp.concatenate(
            [jnp.concatenate([a0, gap], axis=0), jnp.concatenate([gap, a1], axis=0)], axis=1)

    for copy in large_in:
        copy.wait()

    def finish(i):
        @pl.when(has_next)
        def _():
            grad_to_prev(i).wait_recv()

        @pl.when(has_prev)
        def _():
            grad_to_next(i).wait_recv()

        part = pl.ds(i * STEP, STEP)
        from_prev = gprev_v[part].astype(F32)
        from_next = gnext_v[part].astype(F32)
        cut = BLOCK - HALO
        grad_v[part, 0:cut] = (center_v[part, 0:cut] + from_prev[:, :cut]).astype(BF16)
        grad_v[part, cut:HALO] = (
            center_v[part, cut:HALO] + from_prev[:, cut:] + from_next[:, : HALO - cut]).astype(BF16)
        grad_v[part, HALO:BLOCK] = (center_v[part, HALO:BLOCK] + from_next[:, HALO - cut :]).astype(BF16)

    def first_pass(i):
        @pl.when(i + AHEAD < chunks)
        def _():
            send_rows(i + AHEAD)

        part = pl.ds(i * STEP, STEP)
        x3 = x_v[part]
        x = x3.reshape(STEP * BLOCK, CH)
        dy = dy_v[part].reshape(STEP * BLOCK, CH)
        query_gate = nn(x, wqg_ref[...])
        q_v[part] = query_gate[:, :CH].astype(BF16).reshape(STEP, BLOCK, CH)
        gate_v[...] = jax.nn.sigmoid(query_gate[:, CH:]).reshape(STEP, BLOCK, CH)
        dgated_v[...] = nt(dy, wo_ref[...]).astype(BF16).reshape(STEP, BLOCK, CH)
        kv_v[part, HALO : HALO + BLOCK] = nn(x, wkv_ref[...]).astype(BF16).reshape(STEP, BLOCK, 2 * CH)

        @pl.when(has_prev)
        def _():
            to_next(i).wait_recv()

        @pl.when(has_next)
        def _():
            to_prev(i).wait_recv()

        lo = lo_v[part].reshape(STEP * HALO, CH)
        hi = hi_v[part].reshape(STEP * HALO, CH)
        kv_v[part, :HALO] = nn(lo, wkv_ref[...]).astype(BF16).reshape(STEP, HALO, 2 * CH)
        kv_v[part, HALO + BLOCK :] = nn(hi, wkv_ref[...]).astype(BF16).reshape(STEP, HALO, 2 * CH)

        for s in range(STEP):
            at = i * STEP + s
            datt = (dgated_v[s].astype(F32) * gate_v[s]).astype(BF16)
            datt_v[at] = datt
            logit_v[s] = nt(kv_v[at, :, :CH], expand(q_v[at]))
            dprob_v[s] = nt(kv_v[at, :, CH:], expand(datt))
        for w in range(2):
            ks = slice(w * WIN, w * WIN + KEYS)
            ls = slice(w * KEYS, (w + 1) * KEYS)
            for s in range(STEP):
                at = i * STEP + s
                score = logit_v[s, ks, ls] * SCALE + bt_v[w]
                e = jnp.exp(score - jnp.max(score, axis=0, keepdims=True))
                p = e * (1.0 / jnp.sum(e, axis=0, keepdims=True))
                t = dprob_v[s, ks, ls] * p
                ds = t - p * jnp.sum(t, axis=0, keepdims=True)
                dbt_v[w] += ds
                prob_v[at, w] = p.astype(BF16)
                dscore_v[at, w] = ds.astype(BF16)
        for s in range(STEP):
            at = i * STEP + s
            gate = gate_v[s]
            mixed = [fold(tn(prob_v[at, w], kv_v[at, w * WIN : w * WIN + KEYS, CH:])) for w in range(2)]
            attended = jnp.concatenate(mixed, axis=0)
            gated_v[s] = (attended * gate).astype(BF16)
            dgate_v[at] = (dgated_v[s].astype(F32) * attended * (gate * (1.0 - gate))).astype(BF16)

        out = x.astype(F32) + nn(gated_v[...].reshape(STEP * BLOCK, CH), wo_ref[...])
        upd_v[part] = out.astype(BF16).reshape(STEP, BLOCK, CH)

    def second_pass(i):
        part = pl.ds(i * STEP, STEP)
        for s in range(STEP):
            at = i * STEP + s
            dkv_v[s, :, :CH] = (nn(both(dscore_v[at, 0], dscore_v[at, 1]), expand(q_v[at])) * SCALE).astype(BF16)
            dkv_v[s, :, CH:] = nn(both(prob_v[at, 0], prob_v[at, 1]), expand(datt_v[at])).astype(BF16)

        glo = nt(dkv_v[:, :HALO].reshape(STEP * HALO, 2 * CH), wkv_ref[...])
        glo_v[part] = glo.astype(BF16).reshape(STEP, HALO, CH)
        ghi = nt(dkv_v[:, HALO + BLOCK :].reshape(STEP * HALO, 2 * CH), wkv_ref[...])
        ghi_v[part] = ghi.astype(BF16).reshape(STEP, HALO, CH)

        @pl.when(has_prev)
        def _():
            grad_to_prev(i).start()

        @pl.when(has_next)
        def _():
            grad_to_next(i).start()

        for s in range(STEP):
            at = i * STEP + s
            for w in range(2):
                dq = fold(tn(dscore_v[at, w], kv_v[at, w * WIN : w * WIN + KEYS, :CH]))
                dq_v[s, w * WIN : (w + 1) * WIN] = (dq * SCALE).astype(BF16)
        dquery = dq_v[...].reshape(STEP * BLOCK, CH)
        dgate = dgate_v[part].reshape(STEP * BLOCK, CH)
        own = nt(dkv_v[:, HALO : HALO + BLOCK].reshape(STEP * BLOCK, 2 * CH), wkv_ref[...])
        own = own + nt(jnp.concatenate([dquery, dgate], axis=1), wqg_ref[...])
        own = own + dy_v[part].reshape(STEP * BLOCK, CH).astype(F32)
        center_v[part] = own.reshape(STEP, BLOCK, CH)

        @pl.when(i >= LAG)
        def _():
            finish(i - LAG)

    def a_copy(peer, slot):
        return pltpu.make_async_remote_copy(
            src_ref=part_a, dst_ref=red_a.at[slot],
            send_sem=a_send.at[peer], recv_sem=a_recv.at[slot],
            device_id=(row, peer), device_id_type=MESH)

    def b_copy(peer, slot):
        return pltpu.make_async_remote_copy(
            src_ref=part_b, dst_ref=red_b.at[slot],
            send_sem=b_send.at[peer], recv_sem=b_recv.at[slot],
            device_id=(peer, col), device_id_type=MESH)

    @pl.loop(0, chunks)
    def _(i):
        first_pass(i)

        @pl.when(i >= DELAY)
        def _():
            second_pass(i - DELAY)

    gap32 = jnp.zeros((WIN, KEYS), F32)
    dbias = jnp.concatenate(
        [jnp.concatenate([dbt_v[0], gap32], axis=0), jnp.concatenate([gap32, dbt_v[1]], axis=0)], axis=1)
    dtable = tn(key_hot32, dbias, HI)[: 3 * TOK]
    by_token = jnp.concatenate(
        [
            jnp.where(query_token == t, dtable[s * TOK : (s + 1) * TOK], 0.0)
            for s in range(3) for t in range(TOK)
        ], axis=0)
    head_row = (iota((8, LANES), 1) % KEYS) // WIN
    to_head = (head_row == iota((8, LANES), 0)).astype(F32)
    dbias_rows = nt(to_head, by_token, HI).astype(BF16).astype(F32)
    normed, rstd = band_normed()
    part_a[...] = nn(dbias_rows, normed, HI)
    red_a[col] = part_a[...]

    @pl.loop(1, cols)
    def _(d):
        a_copy(lax.rem(col + d, cols), col).start()

    weight = jnp.concatenate([pwt_v[...], jnp.zeros((8 - HEADS, CH), F32)], axis=0)
    dnormed = tn(dbias_rows, weight, HI)
    dvalues = rstd * (
        dnormed - jnp.mean(dnormed, axis=1, keepdims=True)
        - normed * jnp.mean(dnormed * normed, axis=1, keepdims=True))
    for s in range(3):
        for t in range(TOK):
            at = (s * TOK + t) * TOK
            bandgrad_v[t, s * TOK : (s + 1) * TOK] = dvalues[at : at + TOK].astype(BF16)

    def send_piece(cond, target, d, wide, first):
        @pl.when(jnp.logical_and(cond, target != col))
        def _():
            piece_copy(target, d, wide, first).start()

        @pl.when(jnp.logical_and(cond, target == col))
        def _():
            piece_v[d + 1] = bandgrad_v[...]

    to_owners(send_piece)

    @pl.loop(chunks - DELAY, chunks - DELAY + HALF)
    def _(i):
        second_pass(i)

    @pl.loop(1, cols)
    def _(d):
        source = lax.rem(col + d, cols)
        a_copy(source, source).wait_recv()

    total = red_a[0]
    for j in range(1, cols):
        total = total + red_a[j]
    part_b[...] = total
    red_b[row] = total

    @pl.loop(1, rows)
    def _(d):
        b_copy(lax.rem(row + d, rows), row).start()

    @pl.loop(chunks - DELAY + HALF, chunks)
    def _(i):
        second_pass(i)

    def place(d, wide, first):
        j = delta + d

        @pl.when(jnp.logical_and(inside(j), j != col))
        def _():
            piece_copy(clamped(j), d, wide, first).wait_recv()

        @pl.when(inside(j))
        def _():
            for s in range(first, first + wide):
                at = pl.ds(pl.multiple_of((d + s - 1) * TOK, TOK), TOK)
                for t in range(TOK):
                    pair_out[clamped(j) * TOK + t, at] = piece_v[d + 1, t, s * TOK : (s + 1) * TOK]

    all_readers(place)

    @pl.loop(chunks - LAG, chunks)
    def _(i):
        finish(i)

    def sent_piece(cond, target, d, wide, first):
        @pl.when(jnp.logical_and(cond, target != col))
        def _():
            piece_copy(target, d, wide, first).wait_send()

    to_owners(sent_piece)
    all_readers(band_sent)

    @pl.loop(0, chunks)
    def _(i):
        @pl.when(has_next)
        def _():
            to_next(i).wait_send()
            grad_to_next(i).wait_send()

        @pl.when(has_prev)
        def _():
            to_prev(i).wait_send()
            grad_to_prev(i).wait_send()

    @pl.loop(1, cols)
    def _(d):
        a_copy(lax.rem(col + d, cols), col).wait_send()

    @pl.loop(1, rows)
    def _(d):
        source = lax.rem(row + d, rows)
        b_copy(source, source).wait_recv()

    total = red_b[0]
    for j in range(1, rows):
        total = total + red_b[j]
    wgrad_out[...] = total

    @pl.loop(1, rows)
    def _(d):
        b_copy(lax.rem(row + d, rows), row).wait_send()


def final_kernel(upd_in, grad_in, pair_in, wsum, upd_out, grad_out, pair_out, wgrad, sems):
    copies = [
        pltpu.make_async_copy(src, dst, sems.at[n])
        for n, (src, dst) in enumerate([(pair_in, pair_out), (upd_in, upd_out), (grad_in, grad_out)])
    ]
    for copy in copies:
        copy.start()
    wgrad[...] = wsum[:HEADS]
    for copy in copies:
        copy.wait()


def on_device(rows, cols, atom_rows, pair_rep, wqg, wkv, wo, pw, counts, token_mask, cotangent):
    samples = atom_rows.shape[0]
    chunks = samples // STEP
    vmem = pl.BlockSpec(memory_space=pltpu.VMEM)
    hbm = pl.BlockSpec(memory_space=pltpu.HBM)
    own = (samples, BLOCK, CH)
    halo = (samples, HALO, CH)
    dma = pltpu.SemaphoreType.DMA
    upd, grad, pair, wsum = pl.pallas_call(
        functools.partial(main_kernel, rows, cols, samples),
        out_shape=(
            jax.ShapeDtypeStruct(own, BF16),
            jax.ShapeDtypeStruct(own, BF16),
            jax.ShapeDtypeStruct(pair_rep.shape, BF16),
            jax.ShapeDtypeStruct((8, CH), F32),
        ),
        in_specs=[hbm] * 9,
        out_specs=(vmem,) * 4,
        scratch_shapes=[
            pltpu.SMEM((TOK, rows * cols), jnp.int32), pltpu.SMEM((rows * cols * TOK,), jnp.int32),
            pltpu.VMEM((CH, 2 * CH), BF16), pltpu.VMEM((CH, 2 * CH), BF16), pltpu.VMEM((CH, CH), BF16),
            pltpu.VMEM((HEADS, CH), F32), pltpu.VMEM((CH, 8), F32),
            pltpu.VMEM(own, BF16), pltpu.VMEM(own, BF16),
            pltpu.VMEM(halo, BF16), pltpu.VMEM(halo, BF16),
            pltpu.VMEM(halo, BF16), pltpu.VMEM(halo, BF16),
            pltpu.VMEM(halo, BF16), pltpu.VMEM(halo, BF16),
            pltpu.VMEM(own, F32),
            pltpu.VMEM((TOK, 3 * TOK, CH), BF16), pltpu.VMEM((TOK, 3 * TOK, CH), BF16),
            pltpu.VMEM((rows + 2, TOK, 3 * TOK, CH), BF16),
            pltpu.VMEM((2, KEYS, KEYS), F32), pltpu.VMEM((2, KEYS, KEYS), F32),
            pltpu.VMEM((samples, EXT, 2 * CH), BF16), pltpu.VMEM((STEP, EXT, 2 * CH), BF16),
            pltpu.VMEM(own, BF16), pltpu.VMEM((STEP, BLOCK, CH), F32),
            pltpu.VMEM((STEP, BLOCK, CH), BF16), pltpu.VMEM((STEP, BLOCK, CH), BF16),
            pltpu.VMEM(own, BF16), pltpu.VMEM((STEP, BLOCK, CH), BF16), pltpu.VMEM(own, BF16),
            pltpu.VMEM((samples, 2, KEYS, KEYS), BF16), pltpu.VMEM((samples, 2, KEYS, KEYS), BF16),
            pltpu.VMEM((STEP, EXT, LANES), F32), pltpu.VMEM((STEP, EXT, LANES), F32),
            pltpu.VMEM((cols, 8, CH), F32), pltpu.VMEM((rows, 8, CH), F32),
            pltpu.VMEM((8, CH), F32), pltpu.VMEM((8, CH), F32),
            dma((8,)),
            dma((chunks,)), dma((chunks,)), dma((chunks,)), dma((chunks,)),
            dma((chunks,)), dma((chunks,)), dma((chunks,)), dma((chunks,)),
            dma((rows + 2,)), dma((2,)), dma((2,)), dma((rows + 2,)),
            dma((cols,)), dma((cols,)), dma((rows,)), dma((rows,)),
        ],
        compiler_params=pltpu.CompilerParams(
            collective_id=0, has_side_effects=True, vmem_limit_bytes=40 * 2**20),
    )(*[
        pltpu.with_memory_space_constraint(array, pltpu.HBM)
        for array in (counts.T, token_mask, atom_rows, pair_rep, wqg, wkv, wo, pw.T, cotangent)
    ])
    upd, grad, pair_grad, wgrad = pl.pallas_call(
        final_kernel,
        out_shape=(
            jax.ShapeDtypeStruct(own, BF16),
            jax.ShapeDtypeStruct(own, BF16),
            jax.ShapeDtypeStruct(pair_rep.shape, BF16),
            jax.ShapeDtypeStruct((HEADS, CH), F32),
        ),
        in_specs=[vmem, vmem, vmem, vmem],
        out_specs=(hbm, hbm, hbm, vmem),
        scratch_shapes=[dma((3,))],
        compiler_params=pltpu.CompilerParams(vmem_limit_bytes=8 * 2**20),
    )(upd, grad, pair, wsum)
    return upd, grad, pair_grad, wgrad.T


def solution(mesh):
    rows, cols = mesh.shape["row"], mesh.shape["col"]
    atoms = P(None, ("row", "col"), None)
    pairs = P("row", "col", None)
    return jax.shard_map(
        functools.partial(on_device, rows, cols),
        mesh=mesh,
        in_specs=(atoms, pairs, P(), P(), P(), P(), P(), P(), atoms),
        out_specs=(atoms, atoms, pairs, P()),
        check_vma=False,
    )
```
